512 devices in a mesh: row: 16 (over x, y_lo), col: 16 (over z, core), dp: 2 (over y_hi).
Axes of the slice: x: 4, y: 8 (y_hi: 2, y_lo: 4; y = y_hi * 4 + y_lo), z: 8, core: 2. Of those that a mesh axis runs over, the one named last changes fastest.
Arguments:
- grad_output: bfloat16 [2, 2048, 8192], P('dp', 'col', 'row'), may hold values from -0.09375 to 0.09375
- block_input: bfloat16 [2, 2048, 8192], P('dp', 'col', 'row'), may hold values from -6 to 6
- query_branch: bfloat16 [2, 2048, 8192], P('dp', 'row', 'col'), may hold values from -6 to 6
- key_branch: bfloat16 [2, 2048, 8192], P('dp', 'row', 'col'), may hold values from -6 to 6
- value_branch: bfloat16 [2, 2048, 8192], P('dp', 'row', 'col'), may hold values from -6 to 6
- out_weight: bfloat16 [8192, 8192], P('row', 'col'), may hold values from -0.0625 to 0.0625
- filters: float32 [512, 128], P('col'), may hold values from -0.5 to 0.5
Outputs:
- out_weight_grad: float32 [8192, 8192], P('row', 'col')
- value_weight_grad: float32 [8192, 8192], P('col', 'row')
- filter_grad: float32 [512, 128], P('col')
The draws below stay inside these ranges and needn't reach their ends.
All inputs are finite; a program needn't handle non-finite values.
Results may differ from the reference program's by a relative error of at most 0.0029.
Values may be sent and summed in bfloat16 or wider, within the bound.
A program may use at most 128 MiB of HBM per device.

```python
import jax
import jax.numpy as jnp
from jax import lax

D = 8192
GROUPS = 512
KLEN = 128
TOKENS = 2048
SEQS = 2


def steps_of(own_key, shape, pieces, least, high):
    factor_of, own = 1.0, jax.random.fold_in(own_key, 6)
    for dim, parts in pieces:
        steps = jnp.exp(jax.random.uniform(jax.random.fold_in(own, dim), (parts,), jnp.float32, least / len(pieces), high / len(pieces)))
        factor_of = factor_of * jnp.repeat(steps, shape[dim] // parts).reshape([-1 if axis == dim else 1 for axis in range(len(shape))])
    return factor_of


def noise(own_key, shape, scale, most, shards=(), held_as=jnp.bfloat16):
    result = jax.random.normal(own_key, shape, jnp.float32) * scale
    if len(shards) > 0:
        result = steps_of(own_key, shape, shards, -0.22, 0.18) * result
    return jnp.clip(result, min=-most, max=most).astype(held_as)


def setup_inputs(seed: int = 0) -> dict:
    key_list = jax.random.split(jax.random.key(seed), 8)
    grad_output = noise(key_list[0], (SEQS, TOKENS, D), 0.015625, 0.09375, ((0, 2), (1, 16), (2, 16)))
    block_input = noise(key_list[1], (SEQS, TOKENS, D), 1.0, 6.0, ((0, 2), (1, 16), (2, 16)))
    query_branch = noise(key_list[2], (SEQS, TOKENS, D), 1.0, 6.0, ((0, 2), (1, 16), (2, 16)))
    key_branch = noise(key_list[3], (SEQS, TOKENS, D), 1.0, 6.0, ((0, 2), (1, 16), (2, 16)))
    value_branch = noise(key_list[4], (SEQS, TOKENS, D), 1.0, 6.0, ((0, 2), (1, 16), (2, 16)))
    out_weight = noise(key_list[5], (D, D), D ** -0.5, 0.0625, ((0, 16), (1, 16)))
    filters = noise(key_list[6], (GROUPS, KLEN), 0.09, 0.5, ((0, 16),), jnp.float32)
    return dict(grad_output=grad_output, block_input=block_input, query_branch=query_branch, key_branch=key_branch, value_branch=value_branch, out_weight=out_weight, filters=filters)


highest = lax.Precision.HIGHEST

def causal_mix(signal, per_channel):
    seqs, length, width = signal.shape
    lag_count = per_channel.shape[1]
    padded = jnp.pad(signal, ((0, 0), (lag_count, 0), (0, 0)))
    anchor = jnp.zeros((), jnp.int32)

    def add_lag(lag, total):
        shift_at = (lag_count - lag).astype(jnp.int32)
        moved = lax.dynamic_slice(padded, (anchor, shift_at, anchor), (seqs, length, width))
        column = lax.dynamic_index_in_dim(per_channel, lag.astype(jnp.int32), 1, keepdims=False)
        return total + column * moved
    return lax.fori_loop(0, lag_count, add_lag, jnp.zeros(signal.shape, jnp.float32))

def later_mix(signal, per_channel):
    seqs, length, width = signal.shape
    lag_count = per_channel.shape[1]
    padded = jnp.pad(signal, ((0, 0), (0, lag_count), (0, 0)))
    anchor = jnp.zeros((), jnp.int32)

    def add_lag(lag, total):
        moved = lax.dynamic_slice(padded, (anchor, lag.astype(jnp.int32), anchor), (seqs, length, width))
        column = lax.dynamic_index_in_dim(per_channel, lag.astype(jnp.int32), 1, keepdims=False)
        return total + column * moved
    return lax.fori_loop(0, lag_count, add_lag, jnp.zeros(signal.shape, jnp.float32))

def taps_grad(delta_mix, mixed, group_size):
    seqs, length, width = mixed.shape
    padded = jnp.pad(mixed, ((0, 0), (KLEN, 0), (0, 0)))
    anchor = jnp.zeros((), jnp.int32)

    def one_lag(lag):
        shift_at = (KLEN - lag).astype(jnp.int32)
        moved = lax.dynamic_slice(padded, (anchor, shift_at, anchor), (seqs, length, width))
        per_chan = lax.optimization_barrier(jnp.sum(delta_mix * moved, axis=(0, 1)))
        return lax.optimization_barrier(jnp.sum(per_chan.reshape(-1, group_size), axis=1))
    return lax.map(one_lag, jnp.arange(KLEN, dtype=jnp.int32)).T

def reference(grad_output, block_input, query_branch, key_branch, value_branch, out_weight, filters):
    group_size = D // GROUPS
    per_channel = jnp.repeat(filters, group_size, axis=0)
    mixed = key_branch.astype(jnp.float32) * value_branch.astype(jnp.float32)
    conv_out = causal_mix(mixed, per_channel)
    gated = (query_branch.astype(jnp.float32) * conv_out).astype(jnp.bfloat16)
    flat_grad = grad_output.reshape(-1, D)
    delta_out = jnp.dot(flat_grad, out_weight, preferred_element_type=jnp.float32).reshape(query_branch.shape)
    delta_mix = delta_out * query_branch.astype(jnp.float32)
    delta_conv = later_mix(delta_mix, per_channel)
    delta_value = (delta_conv * key_branch.astype(jnp.float32)).astype(jnp.bfloat16)
    filter_grad = taps_grad(delta_mix, mixed, group_size)
    out_weight_grad = jnp.dot(flat_grad.T, gated.reshape(-1, D), preferred_element_type=jnp.float32)
    value_weight_grad = jnp.dot(delta_value.reshape(-1, D).T, block_input.reshape(-1, D), preferred_element_type=jnp.float32)
    return (out_weight_grad, value_weight_grad, filter_grad)
```

```python
import jax
import jax.numpy as jnp
from jax import lax
from jax.experimental import pallas as pl
from jax.experimental.pallas import tpu as pltpu
from jax.sharding import PartitionSpec as P

MESH = pl.DeviceIdType.MESH
F32 = jnp.float32
BF16 = jnp.bfloat16
NX, NYL, NY, NZ = 4, 4, 8, 8
BLK = 16
TOK = 128
SUB = 32
H0 = 9
SEMS = 94


def exact_dot(a, b, dims):
    return lax.dot_general(a, b, (dims, ((), ())), precision=lax.Precision.HIGHEST, preferred_element_type=F32)


def skew(rows, left):
    which = lax.broadcasted_iota(jnp.int32, rows.shape, 0)
    n = rows.shape[1]
    for bit in range(7):
        step = n - (1 << bit) if left else 1 << bit
        rows = jnp.where(((which >> bit) & 1) == 1, pltpu.roll(rows, step, 1), rows)
    return rows


def kernel(
    g_hbm, i_hbm, q_ref, k_ref, v_ref, w_ref, f_ref,
    out_ref, val_ref, tap_ref,
    xa, wt, t3, qkv, gat, dlv, part, r1, r2, ry, acc, fown, fall,
    loc_sem, a2a_send, a2a_recv, tap_send, tap_recv, send_sem, recv_sem,
):
    row, col, dp = lax.axis_index("row"), lax.axis_index("col"), lax.axis_index("dp")
    X, YL, Z, K = lax.div(row, NYL), lax.rem(row, NYL), lax.div(col, 2), lax.rem(col, 2)
    Y = dp * NYL + YL

    def at(x, y, z, k):
        return {"row": x * NYL + lax.rem(y, NYL), "col": z * 2 + k, "dp": lax.div(y, NYL)}

    def wx(d):
        return lax.rem(X + (d + NX), NX)

    def wy(d):
        return lax.rem(Y + (d + NY), NY)

    def wz(d):
        return lax.rem(Z + (d + NZ), NZ)

    xp, xm = at(wx(1), Y, Z, K), at(wx(-1), Y, Z, K)
    yp, ym = at(X, wy(1), Z, K), at(X, wy(-1), Z, K)
    zp, zm = at(X, Y, wz(1), K), at(X, Y, wz(-1), K)
    mate = at(X, Y, Z, 1 - K)
    twin = at(X, wy(4), Z, K)

    copies = []

    def send(src, dst, to):
        n = len(copies)
        c = pltpu.make_async_remote_copy(src, dst, send_sem.at[n], recv_sem.at[n], device_id=to, device_id_type=MESH)
        c.start()
        copies.append(c)
        return c

    own_g = pltpu.make_async_copy(g_hbm.at[0], xa.at[0, col], loc_sem.at[0])
    own_i = pltpu.make_async_copy(i_hbm.at[0], xa.at[2, col], loc_sem.at[1])
    own_g.start()
    own_i.start()

    barrier = pltpu.get_barrier_semaphore()
    me = row * 2 + dp

    def group_peer(s):
        other = lax.rem(me + s, 32)
        return {"row": lax.div(other, 2), "col": col, "dp": lax.rem(other, 2)}

    @pl.loop(1, 32)
    def _(s):
        pl.semaphore_signal(barrier, inc=1, device_id=group_peer(s), device_id_type=MESH)

    for other in (zp, zm, mate):
        pl.semaphore_signal(barrier, inc=1, device_id=other, device_id_type=MESH)

    for n, ref in enumerate((q_ref, k_ref, v_ref)):
        t3[:, n] = ref[0].astype(F32).T.astype(BF16).reshape(BLK, SUB, TOK)
    own_g.wait()
    own_i.wait()
    pl.semaphore_wait(barrier, 34)

    def ring_z(lo, n):
        def s(z):
            return xa.at[pl.ds(lo, n), z * 2 + K]

        def half(z, h):
            return xa.at[pl.ds(lo, n), z * 2 + K, pl.ds(h * 64, 64)]

        mates = []
        ups, downs = [], []
        for step in range(3):
            up, down = s(wz(-step)), s(wz(step))
            ups.append(send(up, up, zp))
            downs.append(send(down, down, zm))
            if step == 0:
                mates.append(send(s(Z), s(Z), mate))
            else:
                mates.append(send(up, up, mate))
                mates.append(send(down, down, mate))
            yield
            ups[-1].wait_recv()
            downs[-1].wait_recv()
        up, down = half(wz(-3), 0), half(wz(3), 1)
        ups.append(send(up, up, zp))
        downs.append(send(down, down, zm))
        for z in (wz(-3), wz(3)):
            mates.append(send(s(z), s(z), mate))
        yield
        ups[-1].wait_recv()
        downs[-1].wait_recv()
        far = s(wz(4))
        mates.append(send(far, far, mate))
        yield
        for c in mates:
            c.wait_recv()

    def gather_xy(buf):
        n1 = BLK - H0

        def c0(y, lo=0, n=H0):
            return buf.at[X, y, pl.ds(lo, n)]

        def c1(x, lo=0, n=n1):
            return buf.at[x, Y, pl.ds(H0 + lo, n)]

        def rows_of(y, lo=0, n=NX):
            return buf.at[pl.ds(lo, n), y, pl.ds(H0, n1)]

        def cols_of(x, lo=0, n=NY):
            return buf.at[x, pl.ds(lo, n), pl.ds(0, H0)]

        def both(up, down, to_up, to_down):
            return send(up, up, to_up), send(down, down, to_down)

        def arrived(pair):
            pair[0].wait_recv()
            pair[1].wait_recv()

        ha, hb = H0 // 2, n1 // 2
        a = both(c0(Y), c0(Y), yp, ym)
        b = both(c1(X), c1(X), xp, xm)
        yield
        arrived(b)
        b = both(c1(wx(-1), 0, hb), c1(wx(1), hb, n1 - hb), xp, xm)
        yield
        arrived(a)
        a = both(c0(wy(-1)), c0(wy(1)), yp, ym)
        yield
        arrived(b)
        b = both(rows_of(Y), rows_of(Y), yp, ym)
        yield
        arrived(a)
        a = both(c0(wy(-2)), c0(wy(2)), yp, ym)
        yield
        arrived(a)
        a = both(c0(wy(-3), 0, ha), c0(wy(3), ha, H0 - ha), yp, ym)
        yield
        arrived(a)
        a = both(cols_of(X), cols_of(X), xp, xm)
        yield
        arrived(b)
        b = both(rows_of(wy(-1)), rows_of(wy(1)), yp, ym)
        yield
        arrived(a)
        a = both(cols_of(wx(-1), 0, 4), cols_of(wx(1), 4, 4), xp, xm)
        yield
        arrived(b)
        b = both(rows_of(wy(-2)), rows_of(wy(2)), yp, ym)
        yield
        arrived(b)
        b = both(rows_of(wy(-3), 0, 2), rows_of(wy(3), 2, 2), yp, ym)
        yield
        arrived(a)
        arrived(b)

    z1 = ring_z(0, 1)
    next(z1)
    tw_g = send(xa.at[0, col], xa.at[1, col], twin)
    tw_i = send(xa.at[2, col], xa.at[3, col], twin)

    qkv[row] = t3[row]

    @pl.loop(1, 16)
    def _(s):
        other = lax.rem(row + s, 16)
        pltpu.make_async_remote_copy(
            t3.at[other], qkv.at[row], a2a_send, a2a_recv,
            device_id={"row": other, "col": col, "dp": dp}, device_id_type=MESH,
        ).start()

    wt[...] = w_ref[...].astype(F32).T.astype(BF16)
    next(z1)

    at_s = lax.broadcasted_iota(jnp.int32, (TOK, TOK), 0)
    at_t = lax.broadcasted_iota(jnp.int32, (TOK, TOK), 1)
    same = at_t >= at_s
    tables = []
    for grp in range(2):
        taps = jnp.broadcast_to(f_ref[pl.ds(row * 2 + grp, 1), :], (TOK, TOK))
        wrapped = skew(taps, False)
        tables.append((jnp.where(same, wrapped, 0.0), jnp.where(same, 0.0, wrapped)))

    next(z1)
    pltpu.make_async_copy(qkv.at[pl.ds(0, 15)], qkv.at[pl.ds(0, 15)], a2a_recv).wait()

    def signal_rows(n, grp):
        return qkv[:, n, pl.ds(16 * grp, 16), :].astype(F32).reshape(BLK * 16, TOK)

    zeros16 = jnp.zeros((16, TOK), F32)
    mixes = []
    for grp in range(2):
        table, before = tables[grp]
        mixed = signal_rows(1, grp) * signal_rows(2, grp)
        earlier = jnp.concatenate([zeros16, mixed[:-16]], axis=0)
        mixes.append((mixed, earlier))
        conv = exact_dot(mixed, table, ((1,), (0,))) + exact_dot(earlier, before, ((1,), (0,)))
        gated = (signal_rows(0, grp) * conv).astype(BF16)
        gat[X, Y, :, pl.ds(16 * grp, 16), :] = gated.reshape(BLK, 16, TOK)
    next(z1)
    ag = gather_xy(gat)
    next(ag)
    next(z1)
    tw_g.wait_recv()
    tw_i.wait_recv()
    z2 = ring_z(1, 3)
    next(z2)
    next(z1, None)

    def product(j):
        left = wt[pl.ds(pl.multiple_of(wx(j) * 128, 128), 128), :]

        @pl.loop(0, 8)
        def _(bp):
            right = xa[0, pl.ds(bp * 2, 2)].reshape(2 * TOK, 512)
            res = lax.dot_general(left, right, (((1,), (1,)), ((), ())), preferred_element_type=F32)
            half, at_blk = lax.div(bp, 4), lax.rem(bp, 4) * 2
            for n in range(2):
                part[j, half, :, at_blk + n] = res[:, n * TOK : (n + 1) * TOK].reshape(NYL, SUB, TOK)

    product(2)
    far_a = send(part.at[2, 0], r1.at[0], xp)
    far_b = send(part.at[2, 1], r1.at[1], xm)
    product(1)
    near_a = send(part.at[1, 1], r2.at[0, 1], xp)
    product(3)
    near_b = send(part.at[3, 0], r2.at[1, 0], xm)
    product(0)
    next(ag)
    next(ag)
    next(ag)
    next(z2)
    far_a.wait_recv()
    part[1, 0] = part[1, 0] + r1[0]
    late_a = send(part.at[1, 0], r2.at[0, 0], xp)
    far_b.wait_recv()
    part[3, 1] = part[3, 1] + r1[1]
    late_b = send(part.at[3, 1], r2.at[1, 1], xm)
    next(ag)
    next(ag)
    next(z2)
    next(ag)
    for c in (near_a, near_b, late_a, late_b):
        c.wait_recv()
    cross = []
    for half in range(2):
        part[0, half] = part[0, half] + (r2[0, half] + r2[1, half])
        for d in range(1, 4):
            peer = lax.rem(YL + d, NYL)
            cross.append(send(part.at[0, half, peer], ry.at[half, d - 1], at(X, dp * NYL + peer, Z, K)))
    next(ag)
    next(z2)
    next(ag)
    for c in cross:
        c.wait_recv()
    summed = []
    for half in range(2):
        summed.append(part[0, half, YL] + ((ry[half, 0] + ry[half, 1]) + ry[half, 2]))
    delta = jnp.concatenate(summed, axis=0)

    tap_rows = []
    for grp in range(2):
        table, before = tables[grp]
        mixed, earlier = mixes[grp]
        delta_mix = delta[:, 16 * grp : 16 * grp + 16].reshape(BLK * 16, TOK) * signal_rows(0, grp)
        later = jnp.concatenate([delta_mix[16:], zeros16], axis=0)
        conv = exact_dot(delta_mix, table, ((1,), (1,))) + exact_dot(later, before, ((1,), (1,)))
        dlv[X, Y, :, pl.ds(16 * grp, 16), :] = (conv * signal_rows(1, grp)).astype(BF16).reshape(BLK, 16, TOK)
        tap_rows.append((delta_mix, mixed, earlier))
    ag2 = gather_xy(dlv)
    next(ag2)
    fown[...] = jnp.zeros_like(fown)
    for grp in range(2):
        delta_mix, mixed, earlier = tap_rows[grp]
        here = exact_dot(mixed.T, delta_mix, ((1,), (0,)))
        there = exact_dot(earlier.T, delta_mix, ((1,), (0,)))
        lags = skew(jnp.where(same, here, there), True)
        fown[pl.ds(grp, 1), :] = jnp.sum(lags, axis=0, keepdims=True)
    mine = dp * 16 + row
    fall[mine] = fown[...]

    @pl.loop(1, 32)
    def _(s):
        pltpu.make_async_remote_copy(
            fown, fall.at[mine], tap_send, tap_recv, device_id=group_peer(s), device_id_type=MESH
        ).start()

    next(ag2)
    next(ag)
    next(ag2)
    next(ag2)
    next(z2)
    next(ag)
    next(ag2)
    next(ag2)
    next(ag, None)
    next(ag2)
    next(z2, None)

    def outer(buf, arr, total):
        total[...] = jnp.zeros_like(total)
        for d in range(2):
            rel = lax.rem(dp + d, 2)

            @pl.loop(0, 4)
            def _(step):
                left = jnp.concatenate(
                    [buf[:, pl.ds(d * NYL, NYL), step * 4 + n].reshape(512, TOK) for n in range(4)], axis=1
                )
                right = xa[arr * 2 + rel, pl.ds(step * 4, 4)].reshape(512, 512)
                total[...] += jnp.dot(left, right, preferred_element_type=F32)

    outer(gat, 0, acc)
    next(ag2)
    out_ref[...] = acc[...].T
    for _ in ag2:
        pass
    outer(dlv, 1, val_ref)

    pltpu.make_async_copy(fall.at[pl.ds(0, 31)], fall.at[pl.ds(0, 31)], tap_recv).wait()
    for r in range(16):
        tap_ref[pl.ds(2 * r, 2), :] = fall[r, 0:2, :] + fall[16 + r, 0:2, :]

    pltpu.make_async_copy(t3.at[pl.ds(0, 15)], t3.at[pl.ds(0, 15)], a2a_send).wait()
    pltpu.make_async_copy(fall.at[pl.ds(0, 31)], fall.at[pl.ds(0, 31)], tap_send).wait()
    for c in copies:
        c.wait_send()


def local(grad_output, block_input, query_branch, key_branch, value_branch, out_weight, filters):
    vmem = pl.BlockSpec(memory_space=pltpu.VMEM)
    hbm = pl.BlockSpec(memory_space=pl.ANY)
    return pl.pallas_call(
        kernel,
        out_shape=(
            jax.ShapeDtypeStruct((512, 512), F32),
            jax.ShapeDtypeStruct((512, 512), F32),
            jax.ShapeDtypeStruct((32, 128), F32),
        ),
        in_specs=[hbm, hbm, vmem, vmem, vmem, vmem, vmem],
        out_specs=(vmem, vmem, vmem),
        scratch_shapes=[
            pltpu.VMEM((4, BLK, TOK, 512), BF16),
            pltpu.VMEM((512, 512), BF16),
            pltpu.VMEM((BLK, 3, SUB, TOK), BF16),
            pltpu.VMEM((BLK, 3, SUB, TOK), BF16),
            pltpu.VMEM((NX, NY, BLK, SUB, TOK), BF16),
            pltpu.VMEM((NX, NY, BLK, SUB, TOK), BF16),
            pltpu.VMEM((NX, 2, NYL, 8, SUB, TOK), F32),
            pltpu.VMEM((2, NYL, 8, SUB, TOK), F32),
            pltpu.VMEM((2, 2, NYL, 8, SUB, TOK), F32),
            pltpu.VMEM((2, 3, 8, SUB, TOK), F32),
            pltpu.VMEM((512, 512), F32),
            pltpu.VMEM((8, 128), F32),
            pltpu.VMEM((32, 8, 128), F32),
            pltpu.SemaphoreType.DMA((2,)),
            pltpu.SemaphoreType.DMA,
            pltpu.SemaphoreType.DMA,
            pltpu.SemaphoreType.DMA,
            pltpu.SemaphoreType.DMA,
            pltpu.SemaphoreType.DMA((SEMS,)),
            pltpu.SemaphoreType.DMA((SEMS,)),
        ],
        compiler_params=pltpu.CompilerParams(collective_id=0, has_side_effects=True, vmem_limit_bytes=60 * 1024 * 1024),
    )(grad_output, block_input, query_branch, key_branch, value_branch, out_weight, filters)


def solution(mesh):
    in_specs = (
        P("dp", "col", "row"),
        P("dp", "col", "row"),
        P("dp", "row", "col"),
        P("dp", "row", "col"),
        P("dp", "row", "col"),
        P("row", "col"),
        P("col", None),
    )
    out_specs = (P("row", "col"), P("col", "row"), P("col", None))
    return jax.shard_map(local, mesh=mesh, in_specs=in_specs, out_specs=out_specs, check_vma=False)
```

```python
import jax
import jax.numpy as jnp
from jax import lax
from jax.experimental import pallas as pl
from jax.experimental.pallas import tpu as pltpu
from jax.sharding import PartitionSpec as P

MESH = pl.DeviceIdType.MESH
F32 = jnp.float32
BF16 = jnp.bfloat16
NX, NYL, NY, NZ = 4, 4, 8, 8
BLK = 16
TOK = 128
SUB = 32
SEMS = 220
AG1 = (10, ((10, 3), (13, 3)))
AG2 = (9, ((9, 4), (13, 3)))
SCHEDULE1 = (
    ("cross", 1), ("late", 3), ("cross", 2), ("cross", 3), ("h0", 1), ("h1", 1), ("h0", 1),
    ("finish", 0), ("finish", 1), ("finish", 2), ("z2", 1), ("finish", 3),
)
SCHEDULE2 = (
    ("g1", 1), ("g0", 1), ("h0", 1), ("h1", 1), ("g0", 1), ("g1", 1), ("h0", 2), ("z2", 1), ("g0", 1), ("h1", 2), ("z2", 1), ("g0", 1), ("g1", 2), ("h0", 1), ("h1", 2), ("taps", 0),
    ("z2", 1), ("g0", 2), ("z2", 1), ("g1", 2), ("h1", 9), ("g0", 2), ("h0", 9), ("z2", 99), ("outer", 0), ("g1", 2), ("g0", 99), ("g1", 99),
)
RDT = BF16


def exact_dot(a, b, dims):
    return lax.dot_general(a, b, (dims, ((), ())), precision=lax.Precision.HIGHEST, preferred_element_type=F32)


def skew(rows, left):
    which = lax.broadcasted_iota(jnp.int32, rows.shape, 0)
    n = rows.shape[1]
    for bit in range(7):
        step = n - (1 << bit) if left else 1 << bit
        rows = jnp.where(((which >> bit) & 1) == 1, pltpu.roll(rows, step, 1), rows)
    return rows


def kernel(
    g_hbm, i_hbm, q_hbm, k_hbm, v_hbm, w_hbm, f_hbm,
    out_ref, val_ref, tap_ref,
    xa, tok, w_ref, f_ref, wt, t3, qkv, gat, dlv, far_out, near_out, late_out, own_sum, r1, r2n, r2l, ry, dsum, acc, fown, fboth, fall,
    loc_sem, a2a_send, a2a_recv, tap_send, tap_recv, send_sem, recv_sem,
):
    row, col, dp = lax.axis_index("row"), lax.axis_index("col"), lax.axis_index("dp")
    X, YL, Z, K = lax.div(row, NYL), lax.rem(row, NYL), lax.div(col, 2), lax.rem(col, 2)
    Y = dp * NYL + YL

    def at(x, y, z, k):
        return {"row": x * NYL + lax.rem(y, NYL), "col": z * 2 + k, "dp": lax.div(y, NYL)}

    def wx(d):
        return lax.rem(X + (d + NX), NX)

    def wy(d):
        return lax.rem(Y + (d + NY), NY)

    def wz(d):
        return lax.rem(Z + (d + NZ), NZ)

    xp, xm = at(wx(1), Y, Z, K), at(wx(-1), Y, Z, K)
    yp, ym = at(X, wy(1), Z, K), at(X, wy(-1), Z, K)
    zp, zm = at(X, Y, wz(1), K), at(X, Y, wz(-1), K)
    mate = at(X, Y, Z, 1 - K)
    twin = at(X, wy(4), Z, K)

    copies = []

    def send(src, dst, to):
        n = len(copies)
        c = pltpu.make_async_remote_copy(src, dst, send_sem.at[n], recv_sem.at[n], device_id=to, device_id_type=MESH)
        c.start()
        copies.append(c)
        return c

    def both(up, down, to_up, to_down):
        return send(up, up, to_up), send(down, down, to_down)

    def arrived(*some):
        for c in some:
            c.wait_recv()

    def run(stream, steps):
        for _ in range(steps):
            next(stream, None)

    own = [
        pltpu.make_async_copy(src, dst, loc_sem.at[n])
        for n, (src, dst) in enumerate((
            (g_hbm.at[0], xa.at[0, col]), (q_hbm.at[0], tok.at[0]), (k_hbm.at[0], tok.at[1]), (v_hbm.at[0], tok.at[2]),
            (i_hbm.at[0], xa.at[2, col]), (w_hbm, w_ref), (f_hbm, f_ref),
        ))
    ]
    for c in own:
        c.start()

    barrier = pltpu.get_barrier_semaphore()
    me = row * 2 + dp

    def group_peer(s):
        other = lax.rem(me + s, 32)
        return {"row": lax.div(other, 2), "col": col, "dp": lax.rem(other, 2)}

    @pl.loop(1, 32)
    def _(s):
        pl.semaphore_signal(barrier, inc=1, device_id=group_peer(s), device_id_type=MESH)

    for other in (zp, zm, mate):
        pl.semaphore_signal(barrier, inc=1, device_id=other, device_id_type=MESH)

    at_s = lax.broadcasted_iota(jnp.int32, (TOK, TOK), 0)
    at_t = lax.broadcasted_iota(jnp.int32, (TOK, TOK), 1)
    same = at_t >= at_s
    for c in own:
        c.wait()
    for n in range(3):
        t3[:, n] = tok[n].astype(F32).T.astype(BF16).reshape(BLK, SUB, TOK)
    qkv[row] = t3[row]
    wt[...] = w_ref[...].astype(F32).T.astype(BF16)
    tables = []
    for grp in range(2):
        taps = jnp.broadcast_to(f_ref[pl.ds(row * 2 + grp, 1), :], (TOK, TOK))
        wrapped = skew(taps, False)
        tables.append((jnp.where(same, wrapped, 0.0), jnp.where(same, 0.0, wrapped)))
    pl.semaphore_wait(barrier, 34)

    mates = {}

    def gather_first():
        def s(z, r):
            return xa.at[0, z * 2 + K, pl.ds(r * 64, 64)]

        def hand(*offsets):
            for o in offsets:
                block = xa.at[0, wz(o) * 2 + K]
                mates[o] = send(block, block, mate)

        pairs = [both(s(Z, r), s(Z, r), zp, zm) for r in range(2)]
        hand(0)
        yield
        for d in (1, 2):
            for r in range(2):
                arrived(*pairs[r])
                pairs[r] = both(s(wz(-d), r), s(wz(d), r), zp, zm)
            hand(-d, d)
            yield
        arrived(*pairs[0])
        up = send(s(wz(-3), 0), s(wz(-3), 0), zp)
        arrived(*pairs[1])
        down = send(s(wz(3), 1), s(wz(3), 1), zm)
        hand(-3, 3)
        yield
        arrived(up, down)
        hand(4)

    def ring_z(lo, n):
        def s(z, first=0, count=TOK):
            return xa.at[pl.ds(lo, n), z * 2 + K, pl.ds(first, count)]

        handed = []
        for step in range(3):
            up, down = s(wz(-step)), s(wz(step))
            pair = both(up, down, zp, zm)
            handed.append(send(up, up, mate))
            if step > 0:
                handed.append(send(down, down, mate))
            yield
            arrived(*pair)
        pair = both(s(wz(-3), 0, 64), s(wz(3), 64, 64), zp, zm)
        for z in (wz(-3), wz(3)):
            handed.append(send(s(z), s(z), mate))
        yield
        arrived(*pair)
        far = s(wz(4))
        handed.append(send(far, far, mate))
        yield
        arrived(*handed)

    def y_first(buf, n0, eager):
        def one(x, o, lo=0, n=n0):
            return buf.at[x, wy(o), pl.ds(lo, n)]

        def cols_of(x, lo=0, n=NY):
            return buf.at[x, pl.ds(lo, n), pl.ds(0, n0)]

        across = {}
        second = []

        def spread(*offsets):
            if eager:
                for o in offsets:
                    across[o] = both(one(X, o), one(X, o), xp, xm)

        def relay(*offsets):
            for o in offsets:
                arrived(*across[o])
                if o in (-1, 0, 2, 4):
                    second.append(send(one(wx(-1), o), one(wx(-1), o), xp))
                else:
                    second.append(send(one(wx(1), o), one(wx(1), o), xm))

        h = n0 // 2
        a = both(one(X, 0), one(X, 0), yp, ym)
        spread(0)
        yield
        for o in (1, 2):
            arrived(*a)
            a = both(one(X, -o), one(X, o), yp, ym)
            spread(-o, o)
            yield
            if eager:
                relay(*((0,) if o == 1 else (-1, 1)))
                yield
        arrived(*a)
        a = both(one(X, -3, 0, h), one(X, 3, h, n0 - h), yp, ym)
        spread(-3, 3)
        yield
        if eager:
            relay(-2, 2)
            yield
        arrived(*a)
        spread(4)
        if eager:
            yield
            relay(-3, 3)
            yield
            relay(4)
            yield
            arrived(*second)
        else:
            yield
            a = both(cols_of(X), cols_of(X), xp, xm)
            yield
            arrived(*a)
            a = both(cols_of(wx(-1), 0, 4), cols_of(wx(1), 4, 4), xp, xm)
            yield
            arrived(*a)

    def x_first(buf, n0, subs):
        n1 = BLK - n0
        h = n1 // 2

        def one(x, lo=0, n=n1):
            return buf.at[x, Y, pl.ds(n0 + lo, n)]

        def rows_of(o, sub, lo=0, n=NX):
            first, count = subs[sub]
            return buf.at[pl.ds(lo, n), wy(o), pl.ds(first, count)]

        b = both(one(X), one(X), xp, xm)
        yield
        arrived(*b)
        b = both(one(wx(-1), 0, h), one(wx(1), h, n1 - h), xp, xm)
        yield
        arrived(*b)
        rings = [both(rows_of(0, n), rows_of(0, n), yp, ym) for n in range(len(subs))]
        yield
        for o in (1, 2, 3):
            for n in range(len(subs)):
                arrived(*rings[n])
                if o < 3:
                    rings[n] = both(rows_of(-o, n), rows_of(o, n), yp, ym)
                else:
                    rings[n] = both(rows_of(-3, n, 0, 2), rows_of(3, n, 2, 2), yp, ym)
                yield
        for n in range(len(subs)):
            arrived(*rings[n])

    offsets = ((0, -1, -2, -3), (1, 2, 3, 4))
    far = [None] * 4
    near = [None] * 4
    late = [None] * 4
    cross = {}

    def product(j, half, p, out):
        left = wt[pl.ds(pl.multiple_of(wx(j) * 128, 128), 128), :]
        right = xa[0, pl.ds(wz(offsets[half][p]) * 2, 2)].reshape(2 * TOK, 512)
        res = lax.dot_general(left, right, (((1,), (1,)), ((), ())), preferred_element_type=F32)
        for n in range(2):
            out[half, p, :, n] = res[:, n * TOK : (n + 1) * TOK].reshape(NYL, SUB, TOK).astype(out.dtype)

    def start_piece(p):
        arrived(mates[offsets[0][p]], mates[offsets[1][p]])
        product(2, 0, p, far_out)
        product(2, 1, p, far_out)
        far[p] = (send(far_out.at[0, p], r1.at[0, p], xp), send(far_out.at[1, p], r1.at[1, p], xm))
        product(1, 1, p, near_out)
        product(3, 0, p, near_out)
        near[p] = (send(near_out.at[1, p], r2n.at[1, p], xp), send(near_out.at[0, p], r2n.at[0, p], xm))
        product(1, 0, p, late_out)
        product(3, 1, p, late_out)
        product(0, 0, p, own_sum)
        product(0, 1, p, own_sum)

    def start_late(p):
        sent = []
        for half, to in ((0, xp), (1, xm)):
            arrived(far[p][half])
            late_out[half, p] = late_out[half, p] + r1[half, p].astype(F32)
            sent.append(send(late_out.at[half, p], r2l.at[half, p], to))
        late[p] = sent

    def start_cross(p):
        arrived(*near[p], *late[p])
        for half in range(2):
            own_sum[half, p] = own_sum[half, p] + (r2n[half, p].astype(F32) + r2l[half, p])
            for d in range(1, 4):
                peer = lax.rem(YL + d, NYL)
                cross[half, p, d] = send(own_sum.at[half, p, peer], ry.at[half, p, d - 1], at(X, dp * NYL + peer, Z, K))

    def finish(p):
        for half in range(2):
            arrived(*[cross[half, p, d] for d in range(1, 4)])
            total = own_sum[half, p, YL] + ((ry[half, p, 0] + ry[half, p, 1]) + ry[half, p, 2])
            dsum[pl.ds(wz(offsets[half][p]) * 2, 2)] = total

    z1 = gather_first()
    run(z1, 1)

    @pl.loop(1, 16)
    def _(s):
        other = lax.rem(row + s, 16)
        pltpu.make_async_remote_copy(
            t3.at[other], qkv.at[row], a2a_send, a2a_recv,
            device_id={"row": other, "col": col, "dp": dp}, device_id_type=MESH,
        ).start()

    tw_g = send(xa.at[0, col], xa.at[1, col], twin)
    tw_i = send(xa.at[2, col], xa.at[3, col], twin)
    run(z1, 1)
    start_piece(0)
    run(z1, 1)
    start_piece(1)
    start_late(0)
    run(z1, 1)
    start_piece(2)
    start_late(1)
    pltpu.make_async_copy(qkv.at[pl.ds(0, 15)], qkv.at[pl.ds(0, 15)], a2a_recv).wait()

    def signal_rows(n, grp):
        return qkv[:, n, pl.ds(16 * grp, 16), :].astype(F32).reshape(BLK * 16, TOK)

    zeros16 = jnp.zeros((16, TOK), F32)
    mixes = []
    for grp in range(2):
        table, before = tables[grp]
        mixed = signal_rows(1, grp) * signal_rows(2, grp)
        earlier = jnp.concatenate([zeros16, mixed[:-16]], axis=0)
        mixes.append((mixed, earlier))
        conv = exact_dot(mixed, table, ((1,), (0,))) + exact_dot(earlier, before, ((1,), (0,)))
        gated = (signal_rows(0, grp) * conv).astype(BF16)
        gat[X, Y, :, pl.ds(16 * grp, 16), :] = gated.reshape(BLK, 16, TOK)
    h0 = y_first(gat, AG1[0], False)
    h1 = x_first(gat, *AG1)
    run(h1, 1)
    run(h0, 1)
    start_cross(0)
    run(z1, 1)
    start_piece(3)
    start_late(2)

    def ring_rest():
        arrived(tw_g, tw_i)
        yield from ring_z(1, 3)

    z2 = ring_rest()
    for stream, steps in SCHEDULE1:
        if stream in ("late", "cross", "finish"):
            {"late": start_late, "cross": start_cross, "finish": finish}[stream](steps)
        else:
            run({"h0": h0, "h1": h1, "z2": z2}[stream], steps)
    delta = dsum[...]

    tap_rows = []
    for grp in range(2):
        table, before = tables[grp]
        mixed, earlier = mixes[grp]
        delta_mix = delta[:, 16 * grp : 16 * grp + 16].reshape(BLK * 16, TOK) * signal_rows(0, grp)
        later = jnp.concatenate([delta_mix[16:], zeros16], axis=0)
        conv = exact_dot(delta_mix, table, ((1,), (1,))) + exact_dot(later, before, ((1,), (1,)))
        dlv[X, Y, :, pl.ds(16 * grp, 16), :] = (conv * signal_rows(1, grp)).astype(BF16).reshape(BLK, 16, TOK)
        tap_rows.append((delta_mix, mixed, earlier))
    g0 = y_first(dlv, AG2[0], True)
    g1 = x_first(dlv, *AG2)
    run(g1, 1)
    run(g0, 1)
    fown[...] = jnp.zeros_like(fown)
    for grp in range(2):
        delta_mix, mixed, earlier = tap_rows[grp]
        here = exact_dot(mixed.T, delta_mix, ((1,), (0,)))
        there = exact_dot(earlier.T, delta_mix, ((1,), (0,)))
        lags = skew(jnp.where(same, here, there), True)
        fown[pl.ds(grp, 1), :] = jnp.sum(lags, axis=0, keepdims=True)
    tap_twin = send(fown, fboth, twin)

    def outer(buf, arr, total):
        total[...] = jnp.zeros_like(total)
        for d in range(2):
            rel = lax.rem(dp + d, 2)

            @pl.loop(0, 4)
            def _(step):
                left = jnp.concatenate(
                    [buf[:, pl.ds(d * NYL, NYL), step * 4 + n].reshape(512, TOK) for n in range(4)], axis=1
                )
                right = xa[arr * 2 + rel, pl.ds(step * 4, 4)].reshape(512, 512)
                total[...] += jnp.dot(left, right, preferred_element_type=F32)

    for stream, steps in SCHEDULE2:
        if stream == "taps":
            arrived(tap_twin)
            fall[row] = fown[...] + fboth[...]

            @pl.loop(1, 16)
            def _(s):
                other = lax.rem(row + s, 16)
                pltpu.make_async_remote_copy(
                    fall.at[row], fall.at[row], tap_send, tap_recv,
                    device_id={"row": other, "col": col, "dp": dp}, device_id_type=MESH,
                ).start()

        elif stream == "outer":
            outer(gat, 0, acc)
            out_ref[...] = acc[...].T
        else:
            run({"h0": h0, "h1": h1, "z2": z2, "g0": g0, "g1": g1}[stream], steps)
    outer(dlv, 1, val_ref)

    pltpu.make_async_copy(fall.at[pl.ds(0, 15)], fall.at[pl.ds(0, 15)], tap_recv).wait()
    for r in range(16):
        tap_ref[pl.ds(2 * r, 2), :] = fall[r, 0:2, :]

    pltpu.make_async_copy(t3.at[pl.ds(0, 15)], t3.at[pl.ds(0, 15)], a2a_send).wait()
    pltpu.make_async_copy(fall.at[pl.ds(0, 15)], fall.at[pl.ds(0, 15)], tap_send).wait()
    for c in copies:
        c.wait_send()


def local(grad_output, block_input, query_branch, key_branch, value_branch, out_weight, filters):
    vmem = pl.BlockSpec(memory_space=pltpu.VMEM)
    hbm = pl.BlockSpec(memory_space=pl.ANY)
    return pl.pallas_call(
        kernel,
        out_shape=(
            jax.ShapeDtypeStruct((512, 512), F32),
            jax.ShapeDtypeStruct((512, 512), F32),
            jax.ShapeDtypeStruct((32, 128), F32),
        ),
        in_specs=[hbm] * 7,
        out_specs=(vmem, vmem, vmem),
        scratch_shapes=[
            pltpu.VMEM((4, BLK, TOK, 512), BF16),
            pltpu.VMEM((3, TOK, 512), BF16),
            pltpu.VMEM((512, 512), BF16),
            pltpu.VMEM((32, 128), F32),
            pltpu.VMEM((512, 512), BF16),
            pltpu.VMEM((BLK, 3, SUB, TOK), BF16),
            pltpu.VMEM((BLK, 3, SUB, TOK), BF16),
            pltpu.VMEM((NX, NY, BLK, SUB, TOK), BF16),
            pltpu.VMEM((NX, NY, BLK, SUB, TOK), BF16),
            pltpu.VMEM((2, 4, NYL, 2, SUB, TOK), RDT),
            pltpu.VMEM((2, 4, NYL, 2, SUB, TOK), RDT),
            pltpu.VMEM((2, 4, NYL, 2, SUB, TOK), F32),
            pltpu.VMEM((2, 4, NYL, 2, SUB, TOK), F32),
            pltpu.VMEM((2, 4, NYL, 2, SUB, TOK), RDT),
            pltpu.VMEM((2, 4, NYL, 2, SUB, TOK), RDT),
            pltpu.VMEM((2, 4, NYL, 2, SUB, TOK), F32),
            pltpu.VMEM((2, 4, 3, 2, SUB, TOK), F32),
            pltpu.VMEM((BLK, SUB, TOK), F32),
            pltpu.VMEM((512, 512), F32),
            pltpu.VMEM((8, 128), F32),
            pltpu.VMEM((8, 128), F32),
            pltpu.VMEM((16, 8, 128), F32),
            pltpu.SemaphoreType.DMA((7,)),
            pltpu.SemaphoreType.DMA,
            pltpu.SemaphoreType.DMA,
            pltpu.SemaphoreType.DMA,
            pltpu.SemaphoreType.DMA,
            pltpu.SemaphoreType.DMA((SEMS,)),
            pltpu.SemaphoreType.DMA((SEMS,)),
        ],
        compiler_params=pltpu.CompilerParams(collective_id=0, has_side_effects=True, vmem_limit_bytes=60 * 1024 * 1024),
    )(grad_output, block_input, query_branch, key_branch, value_branch, out_weight, filters)


def solution(mesh):
    in_specs = (
        P("dp", "col", "row"),
        P("dp", "col", "row"),
        P("dp", "row", "col"),
        P("dp", "row", "col"),
        P("dp", "row", "col"),
        P("row", "col"),
        P("col", None),
    )
    out_specs = (P("row", "col"), P("col", "row"), P("col", None))
    return jax.shard_map(local, mesh=mesh, in_specs=in_specs, out_specs=out_specs, check_vma=False)
```

```python
import jax
import jax.numpy as jnp
from jax import lax
from jax.experimental import pallas as pl
from jax.experimental.pallas import tpu as pltpu
from jax.sharding import PartitionSpec as P

MESH = pl.DeviceIdType.MESH
F32 = jnp.float32
BF16 = jnp.bfloat16
NX, NYL, NY, NZ = 4, 4, 8, 8
BLK = 16
TOK = 128
SUB = 32
SEMS = 220
AG1 = (10, ((10, 3), (13, 3)))
AG2 = (10, ((10, 3), (13, 3)))
SCHEDULE1 = (("cross", 1), ("late", 3), ("cross", 2), ("cross", 3), ("h0", 1), ("h1", 1), ("h0", 1), ("finish", 0), ("finish", 1), ("finish", 2), ("z2", 1), ("finish", 3),)
SCHEDULE2 = (("g1", 1), ("g0", 1), ("h0", 1), ("h1", 1), ("g0", 1), ("g1", 1), ("h0", 2), ("z2", 1), ("g0", 1), ("h1", 2), ("z2", 1), ("g0", 1), ("g1", 2), ("h0", 1), ("h1", 2), ("taps", 0), ("z2", 1), ("g0", 2), ("z2", 1), ("g1", 2), ("h1", 9), ("g0", 2), ("h0", 9), ("z2", 99), ("outer", 0), ("g1", 2), ("g0", 99), ("g1", 99),)
RDT = BF16
NARROW = (2,)


def exact_dot(a, b, dims):
    return lax.dot_general(a, b, (dims, ((), ())), precision=lax.Precision.HIGHEST, preferred_element_type=F32)


def skew(rows, left):
    which = lax.broadcasted_iota(jnp.int32, rows.shape, 0)
    n = rows.shape[1]
    for bit in range(7):
        step = n - (1 << bit) if left else 1 << bit
        rows = jnp.where(((which >> bit) & 1) == 1, pltpu.roll(rows, step, 1), rows)
    return rows


def kernel(
    g_hbm, i_hbm, q_hbm, k_hbm, v_hbm, w_hbm, f_hbm,
    out_ref, val_ref, tap_ref,
    xa, tok, w_ref, f_ref, wt, t3, qkv, gat, dlv, far_out, near_out, late_out, own_sum, r1, r2n, r2l, own_b, ryb, ry, dsum, acc, fown, fboth, fall,
    loc_sem, a2a_send, a2a_recv, tap_send, tap_recv, send_sem, recv_sem,
):
    row, col, dp = lax.axis_index("row"), lax.axis_index("col"), lax.axis_index("dp")
    X, YL, Z, K = lax.div(row, NYL), lax.rem(row, NYL), lax.div(col, 2), lax.rem(col, 2)
    Y = dp * NYL + YL

    def at(x, y, z, k):
        return {"row": x * NYL + lax.rem(y, NYL), "col": z * 2 + k, "dp": lax.div(y, NYL)}

    def wx(d):
        return lax.rem(X + (d + NX), NX)

    def wy(d):
        return lax.rem(Y + (d + NY), NY)

    def wz(d):
        return lax.rem(Z + (d + NZ), NZ)

    xp, xm = at(wx(1), Y, Z, K), at(wx(-1), Y, Z, K)
    yp, ym = at(X, wy(1), Z, K), at(X, wy(-1), Z, K)
    zp, zm = at(X, Y, wz(1), K), at(X, Y, wz(-1), K)
    mate = at(X, Y, Z, 1 - K)
    twin = at(X, wy(4), Z, K)

    copies = []

    def send(src, dst, to):
        n = len(copies)
        c = pltpu.make_async_remote_copy(src, dst, send_sem.at[n], recv_sem.at[n], device_id=to, device_id_type=MESH)
        c.start()
        copies.append(c)
        return c

    def both(up, down, to_up, to_down):
        return send(up, up, to_up), send(down, down, to_down)

    def arrived(*some):
        for c in some:
            c.wait_recv()

    def run(stream, steps):
        for _ in range(steps):
            next(stream, None)

    own = [
        pltpu.make_async_copy(src, dst, loc_sem.at[n])
        for n, (src, dst) in enumerate((
            (g_hbm.at[0], xa.at[0, col]), (q_hbm.at[0], tok.at[0]), (k_hbm.at[0], tok.at[1]), (v_hbm.at[0], tok.at[2]),
            (i_hbm.at[0], xa.at[2, col]), (w_hbm, w_ref), (f_hbm, f_ref),
        ))
    ]
    for c in own:
        c.start()

    barrier = pltpu.get_barrier_semaphore()
    me = row * 2 + dp

    def group_peer(s):
        other = lax.rem(me + s, 32)
        return {"row": lax.div(other, 2), "col": col, "dp": lax.rem(other, 2)}

    @pl.loop(1, 32)
    def _(s):
        pl.semaphore_signal(barrier, inc=1, device_id=group_peer(s), device_id_type=MESH)

    for other in (zp, zm, mate):
        pl.semaphore_signal(barrier, inc=1, device_id=other, device_id_type=MESH)

    at_s = lax.broadcasted_iota(jnp.int32, (TOK, TOK), 0)
    at_t = lax.broadcasted_iota(jnp.int32, (TOK, TOK), 1)
    same = at_t >= at_s
    for c in own:
        c.wait()
    for n in range(3):
        t3[:, n] = tok[n].astype(F32).T.astype(BF16).reshape(BLK, SUB, TOK)
    qkv[row] = t3[row]
    wt[...] = w_ref[...].astype(F32).T.astype(BF16)
    tables = []
    for grp in range(2):
        taps = jnp.broadcast_to(f_ref[pl.ds(row * 2 + grp, 1), :], (TOK, TOK))
        wrapped = skew(taps, False)
        tables.append((jnp.where(same, wrapped, 0.0), jnp.where(same, 0.0, wrapped)))
    pl.semaphore_wait(barrier, 34)

    mates = {}

    def gather_first():
        def s(z, r):
            return xa.at[0, z * 2 + K, pl.ds(r * 64, 64)]

        def hand(*offsets):
            for o in offsets:
                block = xa.at[0, wz(o) * 2 + K]
                mates[o] = send(block, block, mate)

        pairs = [both(s(Z, r), s(Z, r), zp, zm) for r in range(2)]
        hand(0)
        yield
        for d in (1, 2):
            for r in range(2):
                arrived(*pairs[r])
                pairs[r] = both(s(wz(-d), r), s(wz(d), r), zp, zm)
            hand(-d, d)
            yield
        arrived(*pairs[0])
        up = send(s(wz(-3), 0), s(wz(-3), 0), zp)
        arrived(*pairs[1])
        down = send(s(wz(3), 1), s(wz(3), 1), zm)
        hand(-3, 3)
        yield
        arrived(up, down)
        hand(4)

    def ring_z(lo, n):
        def s(z, first=0, count=TOK):
            return xa.at[pl.ds(lo, n), z * 2 + K, pl.ds(first, count)]

        handed = []
        for step in range(3):
            up, down = s(wz(-step)), s(wz(step))
            pair = both(up, down, zp, zm)
            handed.append(send(up, up, mate))
            if step > 0:
                handed.append(send(down, down, mate))
            yield
            arrived(*pair)
        pair = both(s(wz(-3), 0, 64), s(wz(3), 64, 64), zp, zm)
        for z in (wz(-3), wz(3)):
            handed.append(send(s(z), s(z), mate))
        yield
        arrived(*pair)
        far = s(wz(4))
        handed.append(send(far, far, mate))
        yield
        arrived(*handed)

    def y_first(buf, n0, eager):
        def one(x, o, lo=0, n=n0):
            return buf.at[x, wy(o), pl.ds(lo, n)]

        def cols_of(x, lo=0, n=NY):
            return buf.at[x, pl.ds(lo, n), pl.ds(0, n0)]

        across = {}
        second = []

        def spread(*offsets):
            if eager:
                for o in offsets:
                    across[o] = both(one(X, o), one(X, o), xp, xm)

        def relay(*offsets):
            for o in offsets:
                arrived(*across[o])
                if o in (-1, 0, 2, 4):
                    second.append(send(one(wx(-1), o), one(wx(-1), o), xp))
                else:
                    second.append(send(one(wx(1), o), one(wx(1), o), xm))

        h = n0 // 2
        a = both(one(X, 0), one(X, 0), yp, ym)
        spread(0)
        yield
        for o in (1, 2):
            arrived(*a)
            a = both(one(X, -o), one(X, o), yp, ym)
            spread(-o, o)
            yield
            if eager:
                relay(*((0,) if o == 1 else (-1, 1)))
                yield
        arrived(*a)
        a = both(one(X, -3, 0, h), one(X, 3, h, n0 - h), yp, ym)
        spread(-3, 3)
        yield
        if eager:
            relay(-2, 2)
            yield
        arrived(*a)
        spread(4)
        if eager:
            yield
            relay(-3, 3)
            yield
            relay(4)
            yield
            arrived(*second)
        else:
            yield
            a = both(cols_of(X), cols_of(X), xp, xm)
            yield
            arrived(*a)
            a = both(cols_of(wx(-1), 0, 4), cols_of(wx(1), 4, 4), xp, xm)
            yield
            arrived(*a)

    def x_first(buf, n0, subs):
        n1 = BLK - n0
        h = n1 // 2

        def one(x, lo=0, n=n1):
            return buf.at[x, Y, pl.ds(n0 + lo, n)]

        def rows_of(o, sub, lo=0, n=NX):
            first, count = subs[sub]
            return buf.at[pl.ds(lo, n), wy(o), pl.ds(first, count)]

        b = both(one(X), one(X), xp, xm)
        yield
        arrived(*b)
        b = both(one(wx(-1), 0, h), one(wx(1), h, n1 - h), xp, xm)
        yield
        arrived(*b)
        rings = [both(rows_of(0, n), rows_of(0, n), yp, ym) for n in range(len(subs))]
        yield
        for o in (1, 2, 3):
            for n in range(len(subs)):
                arrived(*rings[n])
                if o < 3:
                    rings[n] = both(rows_of(-o, n), rows_of(o, n), yp, ym)
                else:
                    rings[n] = both(rows_of(-3, n, 0, 2), rows_of(3, n, 2, 2), yp, ym)
                yield
        for n in range(len(subs)):
            arrived(*rings[n])

    offsets = ((0, -1, -2, -3), (1, 2, 3, 4))
    far = [None] * 4
    near = [None] * 4
    late = [None] * 4
    cross = {}

    def product(j, half, p, out):
        left = wt[pl.ds(pl.multiple_of(wx(j) * 128, 128), 128), :]
        right = xa[0, pl.ds(wz(offsets[half][p]) * 2, 2)].reshape(2 * TOK, 512)
        res = lax.dot_general(left, right, (((1,), (1,)), ((), ())), preferred_element_type=F32)
        for n in range(2):
            out[half, p, :, n] = res[:, n * TOK : (n + 1) * TOK].reshape(NYL, SUB, TOK).astype(out.dtype)

    def start_piece(p):
        arrived(mates[offsets[0][p]], mates[offsets[1][p]])
        product(2, 0, p, far_out)
        product(2, 1, p, far_out)
        far[p] = (send(far_out.at[0, p], r1.at[0, p], xp), send(far_out.at[1, p], r1.at[1, p], xm))
        product(1, 1, p, near_out)
        product(3, 0, p, near_out)
        near[p] = (send(near_out.at[1, p], r2n.at[1, p], xp), send(near_out.at[0, p], r2n.at[0, p], xm))
        product(1, 0, p, late_out)
        product(3, 1, p, late_out)
        product(0, 0, p, own_sum)
        product(0, 1, p, own_sum)

    def start_late(p):
        sent = []
        for half, to in ((0, xp), (1, xm)):
            arrived(far[p][half])
            late_out[half, p] = late_out[half, p] + r1[half, p].astype(F32)
            sent.append(send(late_out.at[half, p], r2l.at[half, p], to))
        late[p] = sent

    def start_cross(p):
        arrived(*near[p], *late[p])
        for half in range(2):
            own_sum[half, p] = own_sum[half, p] + (r2n[half, p].astype(F32) + r2l[half, p])
            if NARROW:
                own_b[half, p] = own_sum[half, p].astype(BF16)
            for d in range(1, 4):
                peer = lax.rem(YL + d, NYL)
                src, dst = (own_b, ryb) if d in NARROW else (own_sum, ry)
                cross[half, p, d] = send(src.at[half, p, peer], dst.at[half, p, d - 1], at(X, dp * NYL + peer, Z, K))

    def finish(p):
        for half in range(2):
            arrived(*[cross[half, p, d] for d in range(1, 4)])
            terms = [(ryb if d in NARROW else ry)[half, p, d - 1].astype(F32) for d in range(1, 4)]
            total = own_sum[half, p, YL] + ((terms[0] + terms[1]) + terms[2])
            dsum[pl.ds(wz(offsets[half][p]) * 2, 2)] = total

    z1 = gather_first()
    run(z1, 1)

    @pl.loop(1, 16)
    def _(s):
        other = lax.rem(row + s, 16)
        pltpu.make_async_remote_copy(
            t3.at[other], qkv.at[row], a2a_send, a2a_recv,
            device_id={"row": other, "col": col, "dp": dp}, device_id_type=MESH,
        ).start()

    tw_g = send(xa.at[0, col], xa.at[1, col], twin)
    tw_i = send(xa.at[2, col], xa.at[3, col], twin)
    run(z1, 1)
    start_piece(0)
    run(z1, 1)
    start_piece(1)
    start_late(0)
    run(z1, 1)
    start_piece(2)
    start_late(1)
    pltpu.make_async_copy(qkv.at[pl.ds(0, 15)], qkv.at[pl.ds(0, 15)], a2a_recv).wait()

    def signal_rows(n, grp):
        return qkv[:, n, pl.ds(16 * grp, 16), :].astype(F32).reshape(BLK * 16, TOK)

    zeros16 = jnp.zeros((16, TOK), F32)
    mixes = []
    for grp in range(2):
        table, before = tables[grp]
        mixed = signal_rows(1, grp) * signal_rows(2, grp)
        earlier = jnp.concatenate([zeros16, mixed[:-16]], axis=0)
        mixes.append((mixed, earlier))
        conv = exact_dot(mixed, table, ((1,), (0,))) + exact_dot(earlier, before, ((1,), (0,)))
        gated = (signal_rows(0, grp) * conv).astype(BF16)
        gat[X, Y, :, pl.ds(16 * grp, 16), :] = gated.reshape(BLK, 16, TOK)
    h0 = y_first(gat, AG1[0], False)
    h1 = x_first(gat, *AG1)
    run(h1, 1)
    run(h0, 1)
    start_cross(0)
    run(z1, 1)
    start_piece(3)
    start_late(2)

    def ring_rest():
        arrived(tw_g, tw_i)
        yield from ring_z(1, 3)

    z2 = ring_rest()
    for stream, steps in SCHEDULE1:
        if stream in ("late", "cross", "finish"):
            {"late": start_late, "cross": start_cross, "finish": finish}[stream](steps)
        else:
            run({"h0": h0, "h1": h1, "z2": z2}[stream], steps)
    delta = dsum[...]

    tap_rows = []
    for grp in range(2):
        table, before = tables[grp]
        mixed, earlier = mixes[grp]
        delta_mix = delta[:, 16 * grp : 16 * grp + 16].reshape(BLK * 16, TOK) * signal_rows(0, grp)
        later = jnp.concatenate([delta_mix[16:], zeros16], axis=0)
        conv = exact_dot(delta_mix, table, ((1,), (1,))) + exact_dot(later, before, ((1,), (1,)))
        dlv[X, Y, :, pl.ds(16 * grp, 16), :] = (conv * signal_rows(1, grp)).astype(BF16).reshape(BLK, 16, TOK)
        tap_rows.append((delta_mix, mixed, earlier))
    g0 = y_first(dlv, AG2[0], True)
    g1 = x_first(dlv, *AG2)
    run(g1, 1)
    run(g0, 1)
    fown[...] = jnp.zeros_like(fown)
    for grp in range(2):
        delta_mix, mixed, earlier = tap_rows[grp]
        here = exact_dot(mixed.T, delta_mix, ((1,), (0,)))
        there = exact_dot(earlier.T, delta_mix, ((1,), (0,)))
        lags = skew(jnp.where(same, here, there), True)
        fown[pl.ds(grp, 1), :] = jnp.sum(lags, axis=0, keepdims=True)
    tap_twin = send(fown, fboth, twin)

    def outer(buf, arr, total):
        total[...] = jnp.zeros_like(total)
        for d in range(2):
            rel = lax.rem(dp + d, 2)

            @pl.loop(0, 4)
            def _(step):
                left = jnp.concatenate(
                    [buf[:, pl.ds(d * NYL, NYL), step * 4 + n].reshape(512, TOK) for n in range(4)], axis=1
                )
                right = xa[arr * 2 + rel, pl.ds(step * 4, 4)].reshape(512, 512)
                total[...] += jnp.dot(left, right, preferred_element_type=F32)

    for stream, steps in SCHEDULE2:
        if stream == "taps":
            arrived(tap_twin)
            fall[row] = fown[...] + fboth[...]

            @pl.loop(1, 16)
            def _(s):
                other = lax.rem(row + s, 16)
                pltpu.make_async_remote_copy(
                    fall.at[row], fall.at[row], tap_send, tap_recv,
                    device_id={"row": other, "col": col, "dp": dp}, device_id_type=MESH,
                ).start()

        elif stream == "outer":
            outer(gat, 0, acc)
            out_ref[...] = acc[...].T
        else:
            run({"h0": h0, "h1": h1, "z2": z2, "g0": g0, "g1": g1}[stream], steps)
    outer(dlv, 1, val_ref)

    pltpu.make_async_copy(fall.at[pl.ds(0, 15)], fall.at[pl.ds(0, 15)], tap_recv).wait()
    for r in range(16):
        tap_ref[pl.ds(2 * r, 2), :] = fall[r, 0:2, :]

    pltpu.make_async_copy(t3.at[pl.ds(0, 15)], t3.at[pl.ds(0, 15)], a2a_send).wait()
    pltpu.make_async_copy(fall.at[pl.ds(0, 15)], fall.at[pl.ds(0, 15)], tap_send).wait()
    for c in copies:
        c.wait_send()


def local(grad_output, block_input, query_branch, key_branch, value_branch, out_weight, filters):
    vmem = pl.BlockSpec(memory_space=pltpu.VMEM)
    hbm = pl.BlockSpec(memory_space=pl.ANY)
    return pl.pallas_call(
        kernel,
        out_shape=(
            jax.ShapeDtypeStruct((512, 512), F32),
            jax.ShapeDtypeStruct((512, 512), F32),
            jax.ShapeDtypeStruct((32, 128), F32),
        ),
        in_specs=[hbm] * 7,
        out_specs=(vmem, vmem, vmem),
        scratch_shapes=[
            pltpu.VMEM((4, BLK, TOK, 512), BF16),
            pltpu.VMEM((3, TOK, 512), BF16),
            pltpu.VMEM((512, 512), BF16),
            pltpu.VMEM((32, 128), F32),
            pltpu.VMEM((512, 512), BF16),
            pltpu.VMEM((BLK, 3, SUB, TOK), BF16),
            pltpu.VMEM((BLK, 3, SUB, TOK), BF16),
            pltpu.VMEM((NX, NY, BLK, SUB, TOK), BF16),
            pltpu.VMEM((NX, NY, BLK, SUB, TOK), BF16),
            pltpu.VMEM((2, 4, NYL, 2, SUB, TOK), RDT),
            pltpu.VMEM((2, 4, NYL, 2, SUB, TOK), RDT),
            pltpu.VMEM((2, 4, NYL, 2, SUB, TOK), F32),
            pltpu.VMEM((2, 4, NYL, 2, SUB, TOK), F32),
            pltpu.VMEM((2, 4, NYL, 2, SUB, TOK), RDT),
            pltpu.VMEM((2, 4, NYL, 2, SUB, TOK), RDT),
            pltpu.VMEM((2, 4, NYL, 2, SUB, TOK), F32),
            pltpu.VMEM((2, 4, NYL, 2, SUB, TOK), BF16),
            pltpu.VMEM((2, 4, 3, 2, SUB, TOK), BF16),
            pltpu.VMEM((2, 4, 3, 2, SUB, TOK), F32),
            pltpu.VMEM((BLK, SUB, TOK), F32),
            pltpu.VMEM((512, 512), F32),
            pltpu.VMEM((8, 128), F32),
            pltpu.VMEM((8, 128), F32),
            pltpu.VMEM((16, 8, 128), F32),
            pltpu.SemaphoreType.DMA((7,)),
            pltpu.SemaphoreType.DMA,
            pltpu.SemaphoreType.DMA,
            pltpu.SemaphoreType.DMA,
            pltpu.SemaphoreType.DMA,
            pltpu.SemaphoreType.DMA((SEMS,)),
            pltpu.SemaphoreType.DMA((SEMS,)),
        ],
        compiler_params=pltpu.CompilerParams(collective_id=0, has_side_effects=True, vmem_limit_bytes=60 * 1024 * 1024),
    )(grad_output, block_input, query_branch, key_branch, value_branch, out_weight, filters)


def solution(mesh):
    in_specs = (
        P("dp", "col", "row"),
        P("dp", "col", "row"),
        P("dp", "row", "col"),
        P("dp", "row", "col"),
        P("dp", "row", "col"),
        P("row", "col"),
        P("col", None),
    )
    out_specs = (P("row", "col"), P("col", "row"), P("col", None))
    return jax.shard_map(local, mesh=mesh, in_specs=in_specs, out_specs=out_specs, check_vma=False)
```

```python
import jax
import jax.numpy as jnp
from jax import lax
from jax.experimental import pallas as pl
from jax.experimental.pallas import tpu as pltpu
from jax.sharding import PartitionSpec as P

MESH = pl.DeviceIdType.MESH
F32 = jnp.float32
BF16 = jnp.bfloat16
NX, NYL, NY, NZ = 4, 4, 8, 8
BLK = 16
TOK = 128
SUB = 32
SEMS = 220
AG1 = (10, ((10, 3), (13, 3)))
AG2 = (10, ((10, 3), (13, 3)))
SCHEDULE1 = (("cross", 1), ("late", 3), ("cross", 2), ("cross", 3), ("h0", 1), ("h1", 1), ("h0", 1), ("finish", 0), ("finish", 1), ("finish", 2), ("z2", 1), ("finish", 3),)
SCHEDULE2 = (("g1", 1), ("g0", 1), ("h0", 1), ("h1", 1), ("g0", 1), ("g1", 1), ("h0", 2), ("z2", 1), ("g0", 1), ("h1", 2), ("z2", 1), ("g0", 1), ("g1", 2), ("h0", 1), ("h1", 2), ("taps", 0), ("z2", 1), ("g0", 2), ("z2", 1), ("g1", 2), ("h1", 2), ("g0", 2), ("g1", 2), ("h1", 9), ("g0", 1), ("h0", 9), ("z2", 99), ("outer", 0), ("g0", 99), ("g1", 99),)
RDT = BF16
NARROW = (2,)


def exact_dot(a, b, dims):
    return lax.dot_general(a, b, (dims, ((), ())), precision=lax.Precision.HIGHEST, preferred_element_type=F32)


def skew(rows, left):
    which = lax.broadcasted_iota(jnp.int32, rows.shape, 0)
    n = rows.shape[1]
    for bit in range(7):
        step = n - (1 << bit) if left else 1 << bit
        rows = jnp.where(((which >> bit) & 1) == 1, pltpu.roll(rows, step, 1), rows)
    return rows


def kernel(
    g_hbm, i_hbm, q_hbm, k_hbm, v_hbm, w_hbm, f_hbm,
    out_ref, val_ref, tap_ref,
    xa, tok, w_ref, f_ref, wt, t3, qkv, gat, dlv, far_out, near_out, late_out, own_sum, r1, r2n, r2l, own_b, ryb, ry, dsum, acc, fown, fboth, fall,
    loc_sem, a2a_send, a2a_recv, tap_send, tap_recv, send_sem, recv_sem,
):
    row, col, dp = lax.axis_index("row"), lax.axis_index("col"), lax.axis_index("dp")
    X, YL, Z, K = lax.div(row, NYL), lax.rem(row, NYL), lax.div(col, 2), lax.rem(col, 2)
    Y = dp * NYL + YL

    def at(x, y, z, k):
        return {"row": x * NYL + lax.rem(y, NYL), "col": z * 2 + k, "dp": lax.div(y, NYL)}

    def wx(d):
        return lax.rem(X + (d + NX), NX)

    def wy(d):
        return lax.rem(Y + (d + NY), NY)

    def wz(d):
        return lax.rem(Z + (d + NZ), NZ)

    xp, xm = at(wx(1), Y, Z, K), at(wx(-1), Y, Z, K)
    xfar = at(wx(2), Y, Z, K)
    yp, ym = at(X, wy(1), Z, K), at(X, wy(-1), Z, K)
    zp, zm = at(X, Y, wz(1), K), at(X, Y, wz(-1), K)
    mate = at(X, Y, Z, 1 - K)
    twin = at(X, wy(4), Z, K)

    copies = []

    def send(src, dst, to):
        n = len(copies)
        c = pltpu.make_async_remote_copy(src, dst, send_sem.at[n], recv_sem.at[n], device_id=to, device_id_type=MESH)
        c.start()
        copies.append(c)
        return c

    def both(up, down, to_up, to_down):
        return send(up, up, to_up), send(down, down, to_down)

    def arrived(*some):
        for c in some:
            c.wait_recv()

    def run(stream, steps):
        for _ in range(steps):
            next(stream, None)

    own = [
        pltpu.make_async_copy(src, dst, loc_sem.at[n])
        for n, (src, dst) in enumerate((
            (g_hbm.at[0], xa.at[0, col]), (q_hbm.at[0], tok.at[0]), (k_hbm.at[0], tok.at[1]), (v_hbm.at[0], tok.at[2]),
            (i_hbm.at[0], xa.at[2, col]), (w_hbm, w_ref), (f_hbm, f_ref),
        ))
    ]
    for c in own:
        c.start()

    barrier = pltpu.get_barrier_semaphore()

    @pl.loop(1, 16)
    def _(s):
        peer = {"row": lax.rem(row + s, 16), "col": col, "dp": dp}
        pl.semaphore_signal(barrier, inc=1, device_id=peer, device_id_type=MESH)

    for other in (twin, yp, ym, zp, zm, mate):
        pl.semaphore_signal(barrier, inc=1, device_id=other, device_id_type=MESH)

    at_s = lax.broadcasted_iota(jnp.int32, (TOK, TOK), 0)
    at_t = lax.broadcasted_iota(jnp.int32, (TOK, TOK), 1)
    same = at_t >= at_s
    for c in own:
        c.wait()
    for n in range(3):
        t3[:, n] = tok[n].astype(F32).T.astype(BF16).reshape(BLK, SUB, TOK)
    qkv[row] = t3[row]
    wt[...] = w_ref[...].astype(F32).T.astype(BF16)
    tables = []
    for grp in range(2):
        taps = jnp.broadcast_to(f_ref[pl.ds(row * 2 + grp, 1), :], (TOK, TOK))
        wrapped = skew(taps, False)
        tables.append((jnp.where(same, wrapped, 0.0), jnp.where(same, 0.0, wrapped)))
    pl.semaphore_wait(barrier, 21)

    mates = {}

    def gather_first():
        def s(z, r):
            return xa.at[0, z * 2 + K, pl.ds(r * 64, 64)]

        def hand(*offsets):
            for o in offsets:
                block = xa.at[0, wz(o) * 2 + K]
                mates[o] = send(block, block, mate)

        pairs = [both(s(Z, r), s(Z, r), zp, zm) for r in range(2)]
        hand(0)
        yield
        for d in (1, 2):
            for r in range(2):
                arrived(*pairs[r])
                pairs[r] = both(s(wz(-d), r), s(wz(d), r), zp, zm)
            hand(-d, d)
            yield
        arrived(*pairs[0])
        up = send(s(wz(-3), 0), s(wz(-3), 0), zp)
        arrived(*pairs[1])
        down = send(s(wz(3), 1), s(wz(3), 1), zm)
        hand(-3, 3)
        yield
        arrived(up, down)
        hand(4)

    def ring_z(lo, n):
        def s(z, first=0, count=TOK):
            return xa.at[pl.ds(lo, n), z * 2 + K, pl.ds(first, count)]

        handed = []
        for step in range(3):
            up, down = s(wz(-step)), s(wz(step))
            pair = both(up, down, zp, zm)
            handed.append(send(up, up, mate))
            if step > 0:
                handed.append(send(down, down, mate))
            yield
            arrived(*pair)
        pair = both(s(wz(-3), 0, 64), s(wz(3), 64, 64), zp, zm)
        for z in (wz(-3), wz(3)):
            handed.append(send(s(z), s(z), mate))
        yield
        arrived(*pair)
        far = s(wz(4))
        handed.append(send(far, far, mate))
        yield
        arrived(*handed)

    def y_first(buf, n0, eager):
        def one(x, o, lo=0, n=n0):
            return buf.at[x, wy(o), pl.ds(lo, n)]

        def cols_of(x, lo=0, n=NY):
            return buf.at[x, pl.ds(lo, n), pl.ds(0, n0)]

        across = {}
        second = []

        def spread(*offsets):
            if eager:
                for o in offsets:
                    across[o] = both(one(X, o), one(X, o), xp, xm)

        def relay(*offsets):
            for o in offsets:
                arrived(*across[o])
                if o in (-1, 0, 2, 4):
                    second.append(send(one(wx(-1), o), one(wx(-1), o), xp))
                else:
                    second.append(send(one(wx(1), o), one(wx(1), o), xm))

        h = n0 // 2
        a = both(one(X, 0), one(X, 0), yp, ym)
        spread(0)
        yield
        for o in (1, 2):
            arrived(*a)
            a = both(one(X, -o), one(X, o), yp, ym)
            spread(-o, o)
            yield
            if eager:
                relay(*((0,) if o == 1 else (-1, 1)))
                yield
        arrived(*a)
        a = both(one(X, -3, 0, h), one(X, 3, h, n0 - h), yp, ym)
        spread(-3, 3)
        yield
        if eager:
            relay(-2, 2)
            yield
        arrived(*a)
        spread(4)
        if eager:
            yield
            relay(-3, 3)
            yield
            relay(4)
            yield
            arrived(*second)
        else:
            yield
            a = both(cols_of(X), cols_of(X), xp, xm)
            yield
            arrived(*a)
            a = both(cols_of(wx(-1), 0, 4), cols_of(wx(1), 4, 4), xp, xm)
            yield
            arrived(*a)

    def x_first(buf, n0, subs):
        n1 = BLK - n0

        def one(x, lo=0, n=n1):
            return buf.at[x, Y, pl.ds(n0 + lo, n)]

        def rows_of(o, sub, lo=0, n=NX):
            first, count = subs[sub]
            return buf.at[pl.ds(lo, n), wy(o), pl.ds(first, count)]

        b = both(one(X), one(X), xp, xm)
        c = send(one(X), one(X), xfar)
        yield
        yield
        arrived(*b, c)
        rings = [both(rows_of(0, n), rows_of(0, n), yp, ym) for n in range(len(subs))]
        yield
        for o in (1, 2, 3):
            for n in range(len(subs)):
                arrived(*rings[n])
                if o < 3:
                    rings[n] = both(rows_of(-o, n), rows_of(o, n), yp, ym)
                else:
                    rings[n] = both(rows_of(-3, n, 0, 2), rows_of(3, n, 2, 2), yp, ym)
                yield
        for n in range(len(subs)):
            arrived(*rings[n])

    offsets = ((0, -1, -2, -3), (1, 2, 3, 4))
    far = [None] * 4
    near = [None] * 4
    late = [None] * 4
    cross = {}

    def product(j, half, p, out):
        left = wt[pl.ds(pl.multiple_of(wx(j) * 128, 128), 128), :]
        right = xa[0, pl.ds(wz(offsets[half][p]) * 2, 2)].reshape(2 * TOK, 512)
        res = lax.dot_general(left, right, (((1,), (1,)), ((), ())), preferred_element_type=F32)
        for n in range(2):
            out[half, p, :, n] = res[:, n * TOK : (n + 1) * TOK].reshape(NYL, SUB, TOK).astype(out.dtype)

    def start_piece(p):
        arrived(mates[offsets[0][p]], mates[offsets[1][p]])
        product(2, 0, p, far_out)
        product(2, 1, p, far_out)
        far[p] = (send(far_out.at[0, p], r1.at[0, p], xp), send(far_out.at[1, p], r1.at[1, p], xm))
        product(1, 1, p, near_out)
        product(3, 0, p, near_out)
        near[p] = (send(near_out.at[1, p], r2n.at[1, p], xp), send(near_out.at[0, p], r2n.at[0, p], xm))
        product(1, 0, p, late_out)
        product(3, 1, p, late_out)
        product(0, 0, p, own_sum)
        product(0, 1, p, own_sum)

    def start_late(p):
        sent = []
        for half, to in ((0, xp), (1, xm)):
            arrived(far[p][half])
            late_out[half, p] = late_out[half, p] + r1[half, p].astype(F32)
            sent.append(send(late_out.at[half, p], r2l.at[half, p], to))
        late[p] = sent

    def start_cross(p):
        arrived(*near[p], *late[p])
        for half in range(2):
            own_sum[half, p] = own_sum[half, p] + (r2n[half, p].astype(F32) + r2l[half, p])
            if NARROW:
                own_b[half, p] = own_sum[half, p].astype(BF16)
            for d in range(1, 4):
                peer = lax.rem(YL + d, NYL)
                src, dst = (own_b, ryb) if d in NARROW else (own_sum, ry)
                cross[half, p, d] = send(src.at[half, p, peer], dst.at[half, p, d - 1], at(X, dp * NYL + peer, Z, K))

    def finish(p):
        for half in range(2):
            arrived(*[cross[half, p, d] for d in range(1, 4)])
            terms = [(ryb if d in NARROW else ry)[half, p, d - 1].astype(F32) for d in range(1, 4)]
            total = own_sum[half, p, YL] + ((terms[0] + terms[1]) + terms[2])
            dsum[pl.ds(wz(offsets[half][p]) * 2, 2)] = total

    z1 = gather_first()
    run(z1, 1)

    @pl.loop(1, 16)
    def _(s):
        other = lax.rem(row + s, 16)
        pltpu.make_async_remote_copy(
            t3.at[other], qkv.at[row], a2a_send, a2a_recv,
            device_id={"row": other, "col": col, "dp": dp}, device_id_type=MESH,
        ).start()

    tw_g = send(xa.at[0, col], xa.at[1, col], twin)
    tw_i = send(xa.at[2, col], xa.at[3, col], twin)
    run(z1, 1)
    start_piece(0)
    run(z1, 1)
    start_piece(1)
    start_late(0)
    run(z1, 1)
    start_piece(2)
    start_late(1)
    pltpu.make_async_copy(qkv.at[pl.ds(0, 15)], qkv.at[pl.ds(0, 15)], a2a_recv).wait()

    def signal_rows(n, grp):
        return qkv[:, n, pl.ds(16 * grp, 16), :].astype(F32).reshape(BLK * 16, TOK)

    zeros16 = jnp.zeros((16, TOK), F32)
    mixes = []
    for grp in range(2):
        table, before = tables[grp]
        mixed = signal_rows(1, grp) * signal_rows(2, grp)
        earlier = jnp.concatenate([zeros16, mixed[:-16]], axis=0)
        mixes.append((mixed, earlier))
        conv = exact_dot(mixed, table, ((1,), (0,))) + exact_dot(earlier, before, ((1,), (0,)))
        gated = (signal_rows(0, grp) * conv).astype(BF16)
        gat[X, Y, :, pl.ds(16 * grp, 16), :] = gated.reshape(BLK, 16, TOK)
    h0 = y_first(gat, AG1[0], False)
    h1 = x_first(gat, *AG1)
    run(h1, 1)
    run(h0, 1)
    start_cross(0)
    run(z1, 1)
    start_piece(3)
    start_late(2)

    def ring_rest():
        arrived(tw_g, tw_i)
        yield from ring_z(1, 3)

    z2 = ring_rest()
    for stream, steps in SCHEDULE1:
        if stream in ("late", "cross", "finish"):
            {"late": start_late, "cross": start_cross, "finish": finish}[stream](steps)
        else:
            run({"h0": h0, "h1": h1, "z2": z2}[stream], steps)
    delta = dsum[...]

    tap_rows = []
    for grp in range(2):
        table, before = tables[grp]
        mixed, earlier = mixes[grp]
        delta_mix = delta[:, 16 * grp : 16 * grp + 16].reshape(BLK * 16, TOK) * signal_rows(0, grp)
        later = jnp.concatenate([delta_mix[16:], zeros16], axis=0)
        conv = exact_dot(delta_mix, table, ((1,), (1,))) + exact_dot(later, before, ((1,), (1,)))
        dlv[X, Y, :, pl.ds(16 * grp, 16), :] = (conv * signal_rows(1, grp)).astype(BF16).reshape(BLK, 16, TOK)
        tap_rows.append((delta_mix, mixed, earlier))
    g0 = y_first(dlv, AG2[0], True)
    g1 = x_first(dlv, *AG2)
    run(g1, 1)
    run(g0, 1)
    fown[...] = jnp.zeros_like(fown)
    for grp in range(2):
        delta_mix, mixed, earlier = tap_rows[grp]
        here = exact_dot(mixed.T, delta_mix, ((1,), (0,)))
        there = exact_dot(earlier.T, delta_mix, ((1,), (0,)))
        lags = skew(jnp.where(same, here, there), True)
        fown[pl.ds(grp, 1), :] = jnp.sum(lags, axis=0, keepdims=True)
    tap_twin = send(fown, fboth, twin)

    def outer(buf, arr, total):
        total[...] = jnp.zeros_like(total)
        for d in range(2):
            rel = lax.rem(dp + d, 2)

            @pl.loop(0, 4)
            def _(step):
                left = jnp.concatenate(
                    [buf[:, pl.ds(d * NYL, NYL), step * 4 + n].reshape(512, TOK) for n in range(4)], axis=1
                )
                right = xa[arr * 2 + rel, pl.ds(step * 4, 4)].reshape(512, 512)
                total[...] += jnp.dot(left, right, preferred_element_type=F32)

    for stream, steps in SCHEDULE2:
        if stream == "taps":
            arrived(tap_twin)
            fall[row] = fown[...] + fboth[...]

            @pl.loop(1, 16)
            def _(s):
                other = lax.rem(row + s, 16)
                pltpu.make_async_remote_copy(
                    fall.at[row], fall.at[row], tap_send, tap_recv,
                    device_id={"row": other, "col": col, "dp": dp}, device_id_type=MESH,
                ).start()

        elif stream == "outer":
            outer(gat, 0, acc)
            out_ref[...] = acc[...].T
        else:
            run({"h0": h0, "h1": h1, "z2": z2, "g0": g0, "g1": g1}[stream], steps)
    outer(dlv, 1, val_ref)

    pltpu.make_async_copy(fall.at[pl.ds(0, 15)], fall.at[pl.ds(0, 15)], tap_recv).wait()
    for r in range(16):
        tap_ref[pl.ds(2 * r, 2), :] = fall[r, 0:2, :]

    pltpu.make_async_copy(t3.at[pl.ds(0, 15)], t3.at[pl.ds(0, 15)], a2a_send).wait()
    pltpu.make_async_copy(fall.at[pl.ds(0, 15)], fall.at[pl.ds(0, 15)], tap_send).wait()
    for c in copies:
        c.wait_send()


def local(grad_output, block_input, query_branch, key_branch, value_branch, out_weight, filters):
    vmem = pl.BlockSpec(memory_space=pltpu.VMEM)
    hbm = pl.BlockSpec(memory_space=pl.ANY)
    return pl.pallas_call(
        kernel,
        out_shape=(
            jax.ShapeDtypeStruct((512, 512), F32),
            jax.ShapeDtypeStruct((512, 512), F32),
            jax.ShapeDtypeStruct((32, 128), F32),
        ),
        in_specs=[hbm] * 7,
        out_specs=(vmem, vmem, vmem),
        scratch_shapes=[
            pltpu.VMEM((4, BLK, TOK, 512), BF16),
            pltpu.VMEM((3, TOK, 512), BF16),
            pltpu.VMEM((512, 512), BF16),
            pltpu.VMEM((32, 128), F32),
            pltpu.VMEM((512, 512), BF16),
            pltpu.VMEM((BLK, 3, SUB, TOK), BF16),
            pltpu.VMEM((BLK, 3, SUB, TOK), BF16),
            pltpu.VMEM((NX, NY, BLK, SUB, TOK), BF16),
            pltpu.VMEM((NX, NY, BLK, SUB, TOK), BF16),
            pltpu.VMEM((2, 4, NYL, 2, SUB, TOK), RDT),
            pltpu.VMEM((2, 4, NYL, 2, SUB, TOK), RDT),
            pltpu.VMEM((2, 4, NYL, 2, SUB, TOK), F32),
            pltpu.VMEM((2, 4, NYL, 2, SUB, TOK), F32),
            pltpu.VMEM((2, 4, NYL, 2, SUB, TOK), RDT),
            pltpu.VMEM((2, 4, NYL, 2, SUB, TOK), RDT),
            pltpu.VMEM((2, 4, NYL, 2, SUB, TOK), F32),
            pltpu.VMEM((2, 4, NYL, 2, SUB, TOK), BF16),
            pltpu.VMEM((2, 4, 3, 2, SUB, TOK), BF16),
            pltpu.VMEM((2, 4, 3, 2, SUB, TOK), F32),
            pltpu.VMEM((BLK, SUB, TOK), F32),
            pltpu.VMEM((512, 512), F32),
            pltpu.VMEM((8, 128), F32),
            pltpu.VMEM((8, 128), F32),
            pltpu.VMEM((16, 8, 128), F32),
            pltpu.SemaphoreType.DMA((7,)),
            pltpu.SemaphoreType.DMA,
            pltpu.SemaphoreType.DMA,
            pltpu.SemaphoreType.DMA,
            pltpu.SemaphoreType.DMA,
            pltpu.SemaphoreType.DMA((SEMS,)),
            pltpu.SemaphoreType.DMA((SEMS,)),
        ],
        compiler_params=pltpu.CompilerParams(collective_id=0, has_side_effects=True, vmem_limit_bytes=60 * 1024 * 1024),
    )(grad_output, block_input, query_branch, key_branch, value_branch, out_weight, filters)


def solution(mesh):
    in_specs = (
        P("dp", "col", "row"),
        P("dp", "col", "row"),
        P("dp", "row", "col"),
        P("dp", "row", "col"),
        P("dp", "row", "col"),
        P("row", "col"),
        P("col", None),
    )
    out_specs = (P("row", "col"), P("col", "row"), P("col", None))
    return jax.shard_map(local, mesh=mesh, in_specs=in_specs, out_specs=out_specs, check_vma=False)
```

```python
import jax
import jax.numpy as jnp
from jax import lax
from jax.experimental import pallas as pl
from jax.experimental.pallas import tpu as pltpu
from jax.sharding import PartitionSpec as P

MESH = pl.DeviceIdType.MESH
F32 = jnp.float32
BF16 = jnp.bfloat16
NX, NYL, NY, NZ = 4, 4, 8, 8
BLK = 16
TOK = 128
SUB = 32
SEMS = 220
AG1 = (10, ((10, 3), (13, 3)))
AG2 = (10, ((10, 3), (13, 3)))
SCHEDULE1 = (("cross", 1), ("late", 3), ("cross", 2), ("cross", 3), ("h0", 1), ("h1", 1), ("h0", 1), ("finish", 0), ("finish", 1), ("finish", 2), ("z2", 1), ("finish", 3),)
SCHEDULE2 = (("g1", 1), ("g0", 1), ("h0", 1), ("h1", 1), ("g0", 1), ("g1", 1), ("h0", 2), ("z2", 1), ("g0", 1), ("h1", 2), ("z2", 1), ("g0", 1), ("g1", 2), ("h0", 1), ("h1", 2), ("taps", 0), ("z2", 1), ("g0", 2), ("z2", 1), ("g1", 2), ("h1", 2), ("g0", 2), ("g1", 2), ("h1", 9), ("g0", 1), ("h0", 9), ("z2", 99), ("outer", 0), ("g0", 99), ("g1", 99),)
RDT = BF16
NARROW = (2,)


def exact_dot(a, b, dims):
    return lax.dot_general(a, b, (dims, ((), ())), precision=lax.Precision.HIGHEST, preferred_element_type=F32)


def skew(rows, left):
    which = lax.broadcasted_iota(jnp.int32, rows.shape, 0)
    n = rows.shape[1]
    for bit in range(7):
        step = n - (1 << bit) if left else 1 << bit
        rows = jnp.where(((which >> bit) & 1) == 1, pltpu.roll(rows, step, 1), rows)
    return rows


def kernel(
    g_hbm, i_hbm, q_hbm, k_hbm, v_hbm, w_hbm, f_hbm,
    out_ref, val_ref, tap_ref,
    xa, tok, w_ref, f_ref, wt, t3, qkv, gat, dlv, far_out, near_out, late_out, own_sum, r1, r2n, r2l, own_b, ryb, ry, dsum, acc, fown, fboth, fall,
    loc_sem, a2a_send, a2a_recv, tap_send, tap_recv, send_sem, recv_sem,
):
    row, col, dp = lax.axis_index("row"), lax.axis_index("col"), lax.axis_index("dp")
    X, YL, Z, K = lax.div(row, NYL), lax.rem(row, NYL), lax.div(col, 2), lax.rem(col, 2)
    Y = dp * NYL + YL

    def at(x, y, z, k):
        return {"row": x * NYL + lax.rem(y, NYL), "col": z * 2 + k, "dp": lax.div(y, NYL)}

    def wx(d):
        return lax.rem(X + (d + NX), NX)

    def wy(d):
        return lax.rem(Y + (d + NY), NY)

    def wz(d):
        return lax.rem(Z + (d + NZ), NZ)

    xp, xm = at(wx(1), Y, Z, K), at(wx(-1), Y, Z, K)
    xfar = at(wx(2), Y, Z, K)
    yp, ym = at(X, wy(1), Z, K), at(X, wy(-1), Z, K)
    zp, zm = at(X, Y, wz(1), K), at(X, Y, wz(-1), K)
    mate = at(X, Y, Z, 1 - K)
    twin = at(X, wy(4), Z, K)

    copies = []

    def send(src, dst, to):
        n = len(copies)
        c = pltpu.make_async_remote_copy(src, dst, send_sem.at[n], recv_sem.at[n], device_id=to, device_id_type=MESH)
        c.start()
        copies.append(c)
        return c

    def both(up, down, to_up, to_down):
        return send(up, up, to_up), send(down, down, to_down)

    def arrived(*some):
        for c in some:
            c.wait_recv()

    def run(stream, steps):
        for _ in range(steps):
            next(stream, None)

    own = [
        pltpu.make_async_copy(src, dst, loc_sem.at[n])
        for n, (src, dst) in enumerate((
            (g_hbm.at[0], xa.at[0, col]), (q_hbm.at[0], tok.at[0]), (k_hbm.at[0], tok.at[1]), (v_hbm.at[0], tok.at[2]),
            (i_hbm.at[0], xa.at[2, col]), (w_hbm, w_ref), (f_hbm, f_ref),
        ))
    ]
    for c in own:
        c.start()

    barrier = pltpu.get_barrier_semaphore()

    @pl.loop(1, 16)
    def _(s):
        peer = {"row": lax.rem(row + s, 16), "col": col, "dp": dp}
        pl.semaphore_signal(barrier, inc=1, device_id=peer, device_id_type=MESH)

    for other in (twin, yp, ym, zp, zm, mate):
        pl.semaphore_signal(barrier, inc=1, device_id=other, device_id_type=MESH)

    at_s = lax.broadcasted_iota(jnp.int32, (TOK, TOK), 0)
    at_t = lax.broadcasted_iota(jnp.int32, (TOK, TOK), 1)
    same = at_t >= at_s
    for c in own:
        c.wait()
    for n in range(3):
        t3[:, n] = tok[n].astype(F32).T.astype(BF16).reshape(BLK, SUB, TOK)
    qkv[row] = t3[row]
    wt[...] = w_ref[...].astype(F32).T.astype(BF16)
    tables = []
    for grp in range(2):
        taps = jnp.broadcast_to(f_ref[pl.ds(row * 2 + grp, 1), :], (TOK, TOK))
        wrapped = skew(taps, False)
        tables.append((jnp.where(same, wrapped, 0.0), jnp.where(same, 0.0, wrapped)))
    pl.semaphore_wait(barrier, 21)

    mates = {}

    def gather_first():
        def s(z, r):
            return xa.at[0, z * 2 + K, pl.ds(r * 64, 64)]

        def hand(*offsets):
            for o in offsets:
                block = xa.at[0, wz(o) * 2 + K]
                mates[o] = send(block, block, mate)

        pairs = [both(s(Z, r), s(Z, r), zp, zm) for r in range(2)]
        hand(0)
        yield
        for d in (1, 2):
            for r in range(2):
                arrived(*pairs[r])
                pairs[r] = both(s(wz(-d), r), s(wz(d), r), zp, zm)
            hand(-d, d)
            yield
        arrived(*pairs[0])
        up = send(s(wz(-3), 0), s(wz(-3), 0), zp)
        arrived(*pairs[1])
        down = send(s(wz(3), 1), s(wz(3), 1), zm)
        hand(-3, 3)
        yield
        arrived(up, down)
        hand(4)

    def ring_z(lo, n):
        def s(z, first=0, count=TOK):
            return xa.at[pl.ds(lo, n), z * 2 + K, pl.ds(first, count)]

        handed = []
        for step in range(3):
            up, down = s(wz(-step)), s(wz(step))
            pair = both(up, down, zp, zm)
            handed.append(send(up, up, mate))
            if step > 0:
                handed.append(send(down, down, mate))
            yield
            arrived(*pair)
        pair = both(s(wz(-3), 0, 64), s(wz(3), 64, 64), zp, zm)
        for z in (wz(-3), wz(3)):
            handed.append(send(s(z), s(z), mate))
        yield
        arrived(*pair)
        far = s(wz(4))
        handed.append(send(far, far, mate))
        yield
        arrived(*handed)

    def y_first(buf, n0, eager):
        def one(x, o, lo=0, n=n0):
            return buf.at[x, wy(o), pl.ds(lo, n)]

        def cols_of(x, lo=0, n=NY):
            return buf.at[x, pl.ds(lo, n), pl.ds(0, n0)]

        across = {}
        second = []

        def spread(*offsets):
            if eager:
                for o in offsets:
                    across[o] = both(one(X, o), one(X, o), xp, xm)

        def relay(*offsets):
            for o in offsets:
                arrived(*across[o])
                if o in (-1, 0, 2, 4):
                    second.append(send(one(wx(-1), o), one(wx(-1), o), xp))
                else:
                    second.append(send(one(wx(1), o), one(wx(1), o), xm))

        h = n0 // 2
        a = both(one(X, 0), one(X, 0), yp, ym)
        spread(0)
        yield
        for o in (1, 2):
            arrived(*a)
            a = both(one(X, -o), one(X, o), yp, ym)
            spread(-o, o)
            yield
            if eager:
                relay(*((0,) if o == 1 else (-1, 1)))
                yield
        arrived(*a)
        a = both(one(X, -3, 0, h), one(X, 3, h, n0 - h), yp, ym)
        spread(-3, 3)
        yield
        if eager:
            relay(-2, 2)
            yield
        arrived(*a)
        spread(4)
        if eager:
            yield
            relay(-3, 3)
            yield
            relay(4)
            yield
            arrived(*second)
        else:
            yield
            a = both(cols_of(X), cols_of(X), xp, xm)
            yield
            arrived(*a)
            a = both(cols_of(wx(-1), 0, 4), cols_of(wx(1), 4, 4), xp, xm)
            yield
            arrived(*a)

    def x_first(buf, n0, subs):
        n1 = BLK - n0

        def one(x, lo=0, n=n1):
            return buf.at[x, Y, pl.ds(n0 + lo, n)]

        def rows_of(o, sub, lo=0, n=NX):
            first, count = subs[sub]
            return buf.at[pl.ds(lo, n), wy(o), pl.ds(first, count)]

        b = both(one(X), one(X), xp, xm)
        c = send(one(X), one(X), xfar)
        yield
        yield
        arrived(*b, c)
        rings = [both(rows_of(0, n), rows_of(0, n), yp, ym) for n in range(len(subs))]
        yield
        for o in (1, 2, 3):
            for n in range(len(subs)):
                arrived(*rings[n])
                if o < 3:
                    rings[n] = both(rows_of(-o, n), rows_of(o, n), yp, ym)
                else:
                    rings[n] = both(rows_of(-3, n, 0, 2), rows_of(3, n, 2, 2), yp, ym)
                yield
        for n in range(len(subs)):
            arrived(*rings[n])

    offsets = ((0, -1, -2, -3), (1, 2, 3, 4))
    far = [[None, None] for _ in range(4)]
    near = [[None, None] for _ in range(4)]
    late = [None] * 4
    cross = {}

    def product(j, half, p, out):
        left = wt[pl.ds(pl.multiple_of(wx(j) * 128, 128), 128), :]
        right = xa[0, pl.ds(wz(offsets[half][p]) * 2, 2)].reshape(2 * TOK, 512)
        res = lax.dot_general(left, right, (((1,), (1,)), ((), ())), preferred_element_type=F32)
        for n in range(2):
            out[half, p, :, n] = res[:, n * TOK : (n + 1) * TOK].reshape(NYL, SUB, TOK).astype(out.dtype)

    def start_half(p, half):
        arrived(mates[offsets[half][p]])
        product(2, half, p, far_out)
        far[p][half] = send(far_out.at[half, p], r1.at[half, p], (xp, xm)[half])
        product((3, 1)[half], half, p, near_out)
        near[p][half] = send(near_out.at[half, p], r2n.at[half, p], (xm, xp)[half])
        product((1, 3)[half], half, p, late_out)
        product(0, half, p, own_sum)

    def start_piece(p):
        start_half(p, 0)
        start_half(p, 1)

    def start_late(p):
        sent = []
        for half, to in ((0, xp), (1, xm)):
            arrived(far[p][half])
            late_out[half, p] = late_out[half, p] + r1[half, p].astype(F32)
            sent.append(send(late_out.at[half, p], r2l.at[half, p], to))
        late[p] = sent

    def start_cross(p):
        arrived(*near[p], *late[p])
        for half in range(2):
            own_sum[half, p] = own_sum[half, p] + (r2n[half, p].astype(F32) + r2l[half, p])
            if NARROW:
                own_b[half, p] = own_sum[half, p].astype(BF16)
            for d in range(1, 4):
                peer = lax.rem(YL + d, NYL)
                src, dst = (own_b, ryb) if d in NARROW else (own_sum, ry)
                cross[half, p, d] = send(src.at[half, p, peer], dst.at[half, p, d - 1], at(X, dp * NYL + peer, Z, K))

    def finish(p):
        for half in range(2):
            arrived(*[cross[half, p, d] for d in range(1, 4)])
            terms = [(ryb if d in NARROW else ry)[half, p, d - 1].astype(F32) for d in range(1, 4)]
            total = own_sum[half, p, YL] + ((terms[0] + terms[1]) + terms[2])
            dsum[pl.ds(wz(offsets[half][p]) * 2, 2)] = total

    z1 = gather_first()
    run(z1, 1)

    @pl.loop(1, 16)
    def _(s):
        other = lax.rem(row + s, 16)
        pltpu.make_async_remote_copy(
            t3.at[other], qkv.at[row], a2a_send, a2a_recv,
            device_id={"row": other, "col": col, "dp": dp}, device_id_type=MESH,
        ).start()

    tw_g = send(xa.at[0, col], xa.at[1, col], twin)
    tw_i = send(xa.at[2, col], xa.at[3, col], twin)
    start_half(0, 0)
    run(z1, 1)
    start_half(0, 1)
    run(z1, 1)
    start_piece(1)
    start_late(0)
    run(z1, 1)
    start_piece(2)
    start_late(1)
    pltpu.make_async_copy(qkv.at[pl.ds(0, 15)], qkv.at[pl.ds(0, 15)], a2a_recv).wait()

    def signal_rows(n, grp):
        return qkv[:, n, pl.ds(16 * grp, 16), :].astype(F32).reshape(BLK * 16, TOK)

    zeros16 = jnp.zeros((16, TOK), F32)
    mixes = []
    for grp in range(2):
        table, before = tables[grp]
        mixed = signal_rows(1, grp) * signal_rows(2, grp)
        earlier = jnp.concatenate([zeros16, mixed[:-16]], axis=0)
        mixes.append((mixed, earlier))
        conv = exact_dot(mixed, table, ((1,), (0,))) + exact_dot(earlier, before, ((1,), (0,)))
        gated = (signal_rows(0, grp) * conv).astype(BF16)
        gat[X, Y, :, pl.ds(16 * grp, 16), :] = gated.reshape(BLK, 16, TOK)
    h0 = y_first(gat, AG1[0], False)
    h1 = x_first(gat, *AG1)
    run(h1, 1)
    run(h0, 1)
    start_cross(0)
    run(z1, 1)
    start_piece(3)
    start_late(2)

    def ring_rest():
        arrived(tw_g, tw_i)
        yield from ring_z(1, 3)

    z2 = ring_rest()
    for stream, steps in SCHEDULE1:
        if stream in ("late", "cross", "finish"):
            {"late": start_late, "cross": start_cross, "finish": finish}[stream](steps)
        else:
            run({"h0": h0, "h1": h1, "z2": z2}[stream], steps)
    delta = dsum[...]

    tap_rows = []
    for grp in range(2):
        table, before = tables[grp]
        mixed, earlier = mixes[grp]
        delta_mix = delta[:, 16 * grp : 16 * grp + 16].reshape(BLK * 16, TOK) * signal_rows(0, grp)
        later = jnp.concatenate([delta_mix[16:], zeros16], axis=0)
        conv = exact_dot(delta_mix, table, ((1,), (1,))) + exact_dot(later, before, ((1,), (1,)))
        dlv[X, Y, :, pl.ds(16 * grp, 16), :] = (conv * signal_rows(1, grp)).astype(BF16).reshape(BLK, 16, TOK)
        tap_rows.append((delta_mix, mixed, earlier))
    g0 = y_first(dlv, AG2[0], True)
    g1 = x_first(dlv, *AG2)
    run(g1, 1)
    run(g0, 1)
    fown[...] = jnp.zeros_like(fown)
    for grp in range(2):
        delta_mix, mixed, earlier = tap_rows[grp]
        here = exact_dot(mixed.T, delta_mix, ((1,), (0,)))
        there = exact_dot(earlier.T, delta_mix, ((1,), (0,)))
        lags = skew(jnp.where(same, here, there), True)
        fown[pl.ds(grp, 1), :] = jnp.sum(lags, axis=0, keepdims=True)
    tap_twin = send(fown, fboth, twin)

    def outer(buf, arr, total):
        total[...] = jnp.zeros_like(total)
        for d in range(2):
            rel = lax.rem(dp + d, 2)

            @pl.loop(0, 4)
            def _(step):
                left = jnp.concatenate(
                    [buf[:, pl.ds(d * NYL, NYL), step * 4 + n].reshape(512, TOK) for n in range(4)], axis=1
                )
                right = xa[arr * 2 + rel, pl.ds(step * 4, 4)].reshape(512, 512)
                total[...] += jnp.dot(left, right, preferred_element_type=F32)

    for stream, steps in SCHEDULE2:
        if stream == "taps":
            arrived(tap_twin)
            fall[row] = fown[...] + fboth[...]

            @pl.loop(1, 16)
            def _(s):
                other = lax.rem(row + s, 16)
                pltpu.make_async_remote_copy(
                    fall.at[row], fall.at[row], tap_send, tap_recv,
                    device_id={"row": other, "col": col, "dp": dp}, device_id_type=MESH,
                ).start()

        elif stream == "outer":
            outer(gat, 0, acc)
            out_ref[...] = acc[...].T
        else:
            run({"h0": h0, "h1": h1, "z2": z2, "g0": g0, "g1": g1}[stream], steps)
    outer(dlv, 1, val_ref)

    pltpu.make_async_copy(fall.at[pl.ds(0, 15)], fall.at[pl.ds(0, 15)], tap_recv).wait()
    for r in range(16):
        tap_ref[pl.ds(2 * r, 2), :] = fall[r, 0:2, :]

    pltpu.make_async_copy(t3.at[pl.ds(0, 15)], t3.at[pl.ds(0, 15)], a2a_send).wait()
    pltpu.make_async_copy(fall.at[pl.ds(0, 15)], fall.at[pl.ds(0, 15)], tap_send).wait()
    for c in copies:
        c.wait_send()


def local(grad_output, block_input, query_branch, key_branch, value_branch, out_weight, filters):
    vmem = pl.BlockSpec(memory_space=pltpu.VMEM)
    hbm = pl.BlockSpec(memory_space=pl.ANY)
    return pl.pallas_call(
        kernel,
        out_shape=(
            jax.ShapeDtypeStruct((512, 512), F32),
            jax.ShapeDtypeStruct((512, 512), F32),
            jax.ShapeDtypeStruct((32, 128), F32),
        ),
        in_specs=[hbm] * 7,
        out_specs=(vmem, vmem, vmem),
        scratch_shapes=[
            pltpu.VMEM((4, BLK, TOK, 512), BF16),
            pltpu.VMEM((3, TOK, 512), BF16),
            pltpu.VMEM((512, 512), BF16),
            pltpu.VMEM((32, 128), F32),
            pltpu.VMEM((512, 512), BF16),
            pltpu.VMEM((BLK, 3, SUB, TOK), BF16),
            pltpu.VMEM((BLK, 3, SUB, TOK), BF16),
            pltpu.VMEM((NX, NY, BLK, SUB, TOK), BF16),
            pltpu.VMEM((NX, NY, BLK, SUB, TOK), BF16),
            pltpu.VMEM((2, 4, NYL, 2, SUB, TOK), RDT),
            pltpu.VMEM((2, 4, NYL, 2, SUB, TOK), RDT),
            pltpu.VMEM((2, 4, NYL, 2, SUB, TOK), F32),
            pltpu.VMEM((2, 4, NYL, 2, SUB, TOK), F32),
            pltpu.VMEM((2, 4, NYL, 2, SUB, TOK), RDT),
            pltpu.VMEM((2, 4, NYL, 2, SUB, TOK), RDT),
            pltpu.VMEM((2, 4, NYL, 2, SUB, TOK), F32),
            pltpu.VMEM((2, 4, NYL, 2, SUB, TOK), BF16),
            pltpu.VMEM((2, 4, 3, 2, SUB, TOK), BF16),
            pltpu.VMEM((2, 4, 3, 2, SUB, TOK), F32),
            pltpu.VMEM((BLK, SUB, TOK), F32),
            pltpu.VMEM((512, 512), F32),
            pltpu.VMEM((8, 128), F32),
            pltpu.VMEM((8, 128), F32),
            pltpu.VMEM((16, 8, 128), F32),
            pltpu.SemaphoreType.DMA((7,)),
            pltpu.SemaphoreType.DMA,
            pltpu.SemaphoreType.DMA,
            pltpu.SemaphoreType.DMA,
            pltpu.SemaphoreType.DMA,
            pltpu.SemaphoreType.DMA((SEMS,)),
            pltpu.SemaphoreType.DMA((SEMS,)),
        ],
        compiler_params=pltpu.CompilerParams(collective_id=0, has_side_effects=True, vmem_limit_bytes=60 * 1024 * 1024),
    )(grad_output, block_input, query_branch, key_branch, value_branch, out_weight, filters)


def solution(mesh):
    in_specs = (
        P("dp", "col", "row"),
        P("dp", "col", "row"),
        P("dp", "row", "col"),
        P("dp", "row", "col"),
        P("dp", "row", "col"),
        P("row", "col"),
        P("col", None),
    )
    out_specs = (P("row", "col"), P("col", "row"), P("col", None))
    return jax.shard_map(local, mesh=mesh, in_specs=in_specs, out_specs=out_specs, check_vma=False)
```
